128 devices in a mesh: req: 8 (over z_lo, y), blk: 16 (over x, z_hi, core).
Axes of the slice: x: 4, y: 4, z: 4 (z_hi: 2, z_lo: 2; z = z_hi * 2 + z_lo), core: 2. Of those that a mesh axis runs over, the one named last changes fastest.
Arguments:
- hyper_state: float32 [128, 4, 2048], P(('req', 'blk')), may hold values from -6 to 6
- lengths: int32 [128], P('req'), may hold values from 1 to 16384
- key_cache: bfloat16 [128, 16, 2052, 128], P('req', 'blk'), may hold values from -360 to 360
- value_cache: bfloat16 [128, 16, 2052, 128], P('req', 'blk'), may hold values from -6 to 6
- attn_in_weight: bfloat16 [3, 2048, 2048], P(None, None, 'blk'), may hold values from -0.125 to 0.125
- attn_out_weight: bfloat16 [2048, 2048], P('blk'), may hold values from -0.125 to 0.125
- w_gate: bfloat16 [2048, 8192], P('req', 'blk'), may hold values from -0.125 to 0.125
- w_up: bfloat16 [2048, 8192], P('req', 'blk'), may hold values from -0.125 to 0.125
- w_down: bfloat16 [8192, 2048], P('blk', 'req'), may hold values from -0.0625 to 0.0625
- width_in: float32 [2, 4], replicated, may hold values from 0.2 to 1
- stream_mix: float32 [2, 4, 4], replicated, may hold values from -0.6 to 0.6
- depth_out: float32 [2, 4], replicated, may hold values from 0.5 to 1.5
Outputs:
- hyper_out: float32 [128, 4, 2048], P(('req', 'blk'))
The draws below stay inside these ranges and needn't reach their ends.
All inputs are finite; a program needn't handle non-finite values.
Results may differ from the reference program's by a relative error of at most 0.023.
Values may be sent and summed in bfloat16 or wider, within the bound.
No kernel may reach another device: no remote copies, remote signals or barrier semaphores. Data moves between devices by JAX's collectives and lax.ppermute only.
A program may use at most 128 MiB of HBM per device.

```python
import math
import jax
import jax.numpy as jnp
from jax import lax

D = 2048
HEADS = 16
HEAD = 128
FF = 8192
STREAMS = 4
MAXLEN = 16385
REQUESTS = 128
SLOTS = 2052


def draw_key_cache(key, part):
    noise = jax.random.normal(key, (REQUESTS, HEADS, SLOTS, HEAD), jnp.float32)
    noise = jnp.clip(noise, -6.0, 6.0)
    factor = 2.5
    return (noise * factor).astype(jnp.bfloat16)


def place_ends(result, stream_key, least, high):
    dims = result.shape
    spot = [jax.random.randint(jax.random.fold_in(stream_key, axis), (), 0, dims[axis]) for axis in range(len(dims))]
    result = result.at[tuple(spot)].set(least)
    longest = dims.index(max(dims))
    spot[longest] = (spot[longest] + 1) % dims[longest]
    return result.at[tuple(spot)].set(high)


def shard_levels(rng, shape, pieces, least, largest):
    def one(position, shards_of):
        heights = jax.random.uniform(jax.random.fold_in(jax.random.fold_in(rng, 6), position), (shards_of,), jnp.float32, least / len(pieces), largest / len(pieces))
        return jnp.repeat(jnp.exp(heights), shape[position] // shards_of).reshape((-1,) + (1,) * (len(shape) - position - 1))

    loudness = one(*pieces[0])
    for cut in pieces[1:]:
        loudness = loudness * one(*cut)
    return loudness


def bell_draw(key, extent, scale, most, shards=(), dtype=jnp.bfloat16):
    array = jax.random.normal(key, extent, jnp.float32) * scale
    if len(shards) > 0:
        array = shard_levels(key, extent, shards, -0.22, 0.18) * array
    return jnp.clip(array, min=-most, max=most).astype(dtype)


def setup_inputs(seed: int = 0) -> dict:
    key_list = jax.random.split(jax.random.key(seed), 13)
    return {
        "hyper_state": bell_draw(key_list[0], (REQUESTS, STREAMS, D), 1.0, 6.0, ((0, 128),), jnp.float32),
        "lengths": place_ends(jax.random.randint(key_list[1], (REQUESTS,), 1, MAXLEN), jax.random.fold_in(key_list[1], 1), 1, MAXLEN - 1).astype(jnp.int32),
        "key_cache": draw_key_cache(jax.random.fold_in(key_list[12], 71), 0),
        "value_cache": bell_draw(key_list[3], (REQUESTS, HEADS, SLOTS, HEAD), 1.0, 6.0, ((0, 8), (1, 16))),
        "attn_in_weight": bell_draw(key_list[4], (3, D, D), D ** -0.5, 0.125, ((2, 16),)),
        "attn_out_weight": bell_draw(key_list[5], (D, D), D ** -0.5, 0.125, ((0, 16),)),
        "w_gate": bell_draw(key_list[6], (D, FF), D ** -0.5, 0.125, ((0, 8), (1, 16))),
        "w_up": bell_draw(key_list[7], (D, FF), D ** -0.5, 0.125, ((0, 8), (1, 16))),
        "w_down": bell_draw(key_list[8], (FF, D), FF ** -0.5, 0.0625, ((0, 16), (1, 8))),
        "width_in": jnp.clip(jax.random.uniform(key_list[9], (2, STREAMS), jnp.float32, 0.2, 1.0), 0.2, 1.0),
        "stream_mix": jnp.clip(jax.random.uniform(key_list[10], (2, STREAMS, STREAMS), jnp.float32, -0.6, 0.6), -0.6, 0.6),
        "depth_out": jnp.clip(jax.random.uniform(key_list[11], (2, STREAMS), jnp.float32, 0.5, 1.5), 0.5, 1.5),
    }


def layer_norm(values):
    center = values - lax.optimization_barrier(jnp.mean(values, axis=-1, keepdims=True))
    spread = lax.optimization_barrier(jnp.mean(center * center, axis=-1, keepdims=True))
    return center * lax.rsqrt(spread + 1e-05)

def combine(state, weights):
    return lax.optimization_barrier(jnp.sum(state * weights[None, :, None], axis=1))

def remix(state, matrix):
    return lax.optimization_barrier(jnp.sum(state[:, :, None, :] * matrix[None, :, :, None], axis=1))

def rotate(values, positions):
    half = values.shape[-1] // 2
    index = jnp.arange(half).astype(jnp.float32)
    freqs = jnp.exp(index * (-2.0 * math.log(10000.0) / values.shape[-1]))
    angles = positions.astype(jnp.float32)[:, None, None] * freqs[None, None, :]
    cosine = jnp.cos(angles)
    sine = jnp.sin(angles)
    first = values[..., :half]
    second = values[..., half:]
    return jnp.concatenate([first * cosine - second * sine, second * cosine + first * sine], axis=-1)

def attend_one(item):
    query, key_new, value_new, keys, values, length = item
    scale = query.shape[-1] ** (-0.5)
    query_wide = query.astype(jnp.float32)
    scores = jnp.einsum('he,hse->hs', query_wide, keys.astype(jnp.float32)) * scale
    own = lax.optimization_barrier(jnp.sum(query_wide * key_new.astype(jnp.float32), axis=-1)) * scale
    valid = jnp.arange(keys.shape[1]).astype(jnp.int32)[None, :] < length
    peak = jnp.maximum(lax.optimization_barrier(jnp.max(jnp.where(valid, scores, -jnp.inf), axis=-1)), own)
    shares = jnp.where(valid, jnp.exp(scores - peak[:, None]), 0.0)
    own_share = jnp.exp(own - peak)
    denom = lax.optimization_barrier(jnp.sum(shares, axis=-1)) + own_share
    probs = (shares / denom[:, None]).astype(jnp.bfloat16)
    own_prob = (own_share / denom).astype(jnp.bfloat16)
    mixed = jnp.einsum('hs,hse->he', probs.astype(jnp.float32), values.astype(jnp.float32))
    mixed = mixed + own_prob.astype(jnp.float32)[:, None] * value_new.astype(jnp.float32)
    return mixed.astype(jnp.bfloat16)

def reference(hyper_state, lengths, key_cache, value_cache, attn_in_weight, attn_out_weight, w_gate, w_up, w_down, width_in, stream_mix, depth_out):
    state = hyper_state
    normed = layer_norm(combine(state, width_in[0])).astype(jnp.bfloat16)
    count = normed.shape[0]
    projected = [jnp.dot(normed, attn_in_weight[index], preferred_element_type=jnp.float32) for index in range(3)]
    query = rotate(projected[0].reshape(count, HEADS, HEAD), lengths).astype(jnp.bfloat16)
    key_new = rotate(projected[1].reshape(count, HEADS, HEAD), lengths).astype(jnp.bfloat16)
    value_new = projected[2].reshape(count, HEADS, HEAD).astype(jnp.bfloat16)
    attended = lax.map(attend_one, (query, key_new, value_new, key_cache, value_cache, lengths))
    flat = attended.reshape(count, HEADS * HEAD)
    attn_out = jnp.dot(flat, attn_out_weight, preferred_element_type=jnp.float32)
    state = remix(state, stream_mix[0]) + depth_out[0][None, :, None] * attn_out[:, None, :]
    normed_mlp = layer_norm(combine(state, width_in[1])).astype(jnp.bfloat16)
    gate = jnp.dot(normed_mlp, w_gate, preferred_element_type=jnp.float32)
    upward = jnp.dot(normed_mlp, w_up, preferred_element_type=jnp.float32)
    hidden = (jax.nn.silu(gate) * upward).astype(jnp.bfloat16)
    mlp_out = jnp.dot(hidden, w_down, preferred_element_type=jnp.float32)
    return remix(state, stream_mix[1]) + depth_out[1][None, :, None] * mlp_out[:, None, :]
```

```python
import math

import jax
import jax.numpy as jnp
from jax import lax
from jax.sharding import PartitionSpec as P


def layer_norm(values):
    center = values - jnp.mean(values, axis=-1, keepdims=True)
    spread = jnp.mean(center * center, axis=-1, keepdims=True)
    return center * lax.rsqrt(spread + 1e-05)


def combine(state, weights):
    return jnp.sum(state * weights[None, :, None], axis=1)


def remix(state, matrix):
    return jnp.sum(state[:, :, None, :] * matrix[None, :, :, None], axis=1)


def rotate(values, positions):
    half = values.shape[-1] // 2
    index = jnp.arange(half).astype(jnp.float32)
    freqs = jnp.exp(index * (-2.0 * math.log(10000.0) / values.shape[-1]))
    angles = positions.astype(jnp.float32)[:, None, None] * freqs[None, None, :]
    cosine = jnp.cos(angles)
    sine = jnp.sin(angles)
    first = values[..., :half]
    second = values[..., half:]
    return jnp.concatenate(
        [first * cosine - second * sine, second * cosine + first * sine], axis=-1
    )


def attend_group(query, key_new, value_new, keys, values, lengths):
    scale = query.shape[-1] ** (-0.5)
    scores = jnp.einsum("rhe,rhse->rhs", query, keys, preferred_element_type=jnp.float32) * scale
    own = jnp.sum(query.astype(jnp.float32) * key_new.astype(jnp.float32), axis=-1) * scale
    valid = jnp.arange(keys.shape[2])[None, None, :] < lengths[:, None, None]
    peak = jnp.maximum(jnp.max(jnp.where(valid, scores, -jnp.inf), axis=-1), own)
    shares = jnp.where(valid, jnp.exp(scores - peak[..., None]), 0.0)
    own_share = jnp.exp(own - peak)
    denom = jnp.sum(shares, axis=-1) + own_share
    probs = (shares / denom[..., None]).astype(jnp.bfloat16)
    own_prob = (own_share / denom).astype(jnp.bfloat16)
    mixed = jnp.einsum("rhs,rhse->rhe", probs, values, preferred_element_type=jnp.float32)
    mixed = mixed + own_prob.astype(jnp.float32)[..., None] * value_new.astype(jnp.float32)
    return mixed.astype(jnp.bfloat16)


def spread(rows, axis):
    copies = jnp.broadcast_to(rows[None], (lax.axis_size(axis),) + rows.shape)
    return lax.all_to_all(copies, axis, split_axis=0, concat_axis=0, tiled=True)


def on_device(
    hyper_state,
    lengths,
    key_cache,
    value_cache,
    attn_in_weight,
    attn_out_weight,
    w_gate,
    w_up,
    w_down,
    width_in,
    stream_mix,
    depth_out,
):
    heads_here = key_cache.shape[1]
    head_size = key_cache.shape[3]
    width = hyper_state.shape[2]
    req_count = lax.axis_size("req")
    blk_count = lax.axis_size("blk")
    both = ("req", "blk")
    normed = layer_norm(combine(hyper_state, width_in[0])).astype(jnp.bfloat16)
    group_rows = spread(normed, "blk").reshape(blk_count, width)
    projected = jnp.einsum(
        "rd,kde->rke", group_rows, attn_in_weight, preferred_element_type=jnp.float32
    )
    group = projected.shape[0]
    query = rotate(projected[:, 0].reshape(group, heads_here, head_size), lengths).astype(
        jnp.bfloat16
    )
    key_new = rotate(projected[:, 1].reshape(group, heads_here, head_size), lengths).astype(
        jnp.bfloat16
    )
    value_new = projected[:, 2].reshape(group, heads_here, head_size).astype(jnp.bfloat16)
    attended = attend_group(query, key_new, value_new, key_cache, value_cache, lengths)
    flat = attended.reshape(group, heads_here * head_size)
    attn_part = jnp.dot(flat, attn_out_weight, preferred_element_type=jnp.float32)
    attn_out = jnp.sum(
        lax.all_to_all(attn_part, "blk", split_axis=0, concat_axis=0, tiled=True),
        axis=0,
        keepdims=True,
    )
    state = remix(hyper_state, stream_mix[0]) + depth_out[0][None, :, None] * attn_out[:, None, :]
    normed_mlp = layer_norm(combine(state, width_in[1])).astype(jnp.bfloat16)
    feature_part = w_gate.shape[0]
    pieces = normed_mlp.reshape(req_count, 1, feature_part)
    pieces = jnp.broadcast_to(pieces, (req_count, blk_count, feature_part))
    columns = lax.all_to_all(
        pieces.reshape(req_count * blk_count, feature_part),
        both,
        split_axis=0,
        concat_axis=0,
        tiled=True,
    )
    hidden_part = w_gate.shape[1]
    gate_part = jnp.dot(columns, w_gate, preferred_element_type=jnp.float32)
    up_part = jnp.dot(columns, w_up, preferred_element_type=jnp.float32)
    parts = jnp.concatenate([gate_part, up_part], axis=1).astype(jnp.bfloat16)
    parts = parts.reshape(req_count, blk_count, 2 * hidden_part)
    parts = lax.all_to_all(parts, "req", split_axis=0, concat_axis=0, tiled=True)
    sums = jnp.sum(parts.astype(jnp.float32), axis=0)
    gate = sums[:, :hidden_part]
    upward = sums[:, hidden_part:]
    hidden = (jax.nn.silu(gate) * upward).astype(jnp.bfloat16)
    hidden_all = spread(hidden, "req").reshape(req_count * blk_count, hidden_part)
    down_part = jnp.dot(hidden_all, w_down, preferred_element_type=jnp.float32)
    down = lax.all_to_all(down_part, both, split_axis=0, concat_axis=0, tiled=True)
    mlp_out = jnp.sum(down.reshape(req_count, blk_count, feature_part), axis=1).reshape(1, width)
    return remix(state, stream_mix[1]) + depth_out[1][None, :, None] * mlp_out[:, None, :]


def solution(mesh):
    placed = (
        P(("req", "blk"), None, None),
        P("req"),
        P("req", "blk", None, None),
        P("req", "blk", None, None),
        P(None, None, "blk"),
        P("blk", None),
        P("req", "blk"),
        P("req", "blk"),
        P("blk", "req"),
        P(),
        P(),
        P(),
    )
    return jax.shard_map(
        on_device,
        mesh=mesh,
        in_specs=placed,
        out_specs=P(("req", "blk"), None, None),
        check_vma=False,
    )
```

```python
import functools
import math

import jax
import jax.numpy as jnp
from jax import lax
from jax.experimental import pallas as pl
from jax.experimental.pallas import tpu as pltpu
from jax.sharding import Mesh, PartitionSpec as P

LANES = 128
FAR_BELOW = -1e30
VMEM = pl.BlockSpec(memory_space=pltpu.VMEM)
SMEM = pl.BlockSpec(memory_space=pltpu.SMEM)
HBM = pl.BlockSpec(memory_space=pl.ANY)


def normalize(values):
    count = values.shape[0] * values.shape[1]
    center = values - jnp.sum(values, keepdims=True) / count
    spread = jnp.sum(center * center, keepdims=True) / count
    return center * lax.rsqrt(spread + 1e-05)


def enter_kernel(state_ref, width_ref, mix_ref, send_ref, mixed_ref, tiles):
    streams, rows = tiles.shape[0], tiles.shape[1]
    for row in range(rows):
        tiles[:, row, :] = state_ref[0, :, row * LANES : (row + 1) * LANES]
    state = [tiles[stream] for stream in range(streams)]
    combined = sum(width_ref[0, stream] * state[stream] for stream in range(streams))
    send_ref[...] = jnp.broadcast_to(normalize(combined)[None], send_ref.shape)
    for target in range(streams):
        mixed_ref[target] = sum(mix_ref[0, stream, target] * state[stream] for stream in range(streams))


def halves_kernel(gate_hbm, up_hbm, down_hbm, own_ref, sent_ref, sems):
    half = own_ref.shape[1]
    side = lax.axis_index("zlo")
    copies = []
    for index, (target, which) in enumerate(((sent_ref, 1 - side), (own_ref, side))):
        begin = pl.multiple_of(which * half, half)
        copies += [
            pltpu.make_async_copy(gate_hbm.at[:, pl.ds(begin, half)], target.at[0], sems.at[3 * index]),
            pltpu.make_async_copy(up_hbm.at[:, pl.ds(begin, half)], target.at[1], sems.at[3 * index + 1]),
            pltpu.make_async_copy(down_hbm.at[pl.ds(begin, half), :], target.at[2], sems.at[3 * index + 2]),
        ]
    for copy in copies:
        copy.start()
    for copy in copies:
        copy.wait()


def attend_kernel(
    rows_ref,
    cos_ref,
    sin_ref,
    length_ref,
    weight_ref,
    keys_hbm,
    values_hbm,
    out_weight_ref,
    send_ref,
    keys,
    values,
    scores,
    key_sems,
    value_sems,
    *,
    pieces,
):
    def copies(source, target, sems):
        return [
            pltpu.make_async_copy(
                source.at[pl.ds(begin, size)], target.at[pl.ds(begin, size)], sems.at[index]
            )
            for index, (begin, size) in enumerate(pieces)
        ]

    key_copies = copies(keys_hbm, keys, key_sems)
    value_copies = copies(values_hbm, values, value_sems)
    for copy in key_copies + value_copies:
        copy.start()

    group = rows_ref.shape[0]
    head = keys.shape[1]
    rows = jnp.concatenate([rows_ref[:, row, :] for row in range(rows_ref.shape[1])], axis=1)
    rows = rows.astype(jnp.bfloat16)
    projected = [
        jnp.dot(rows, weight_ref[index], preferred_element_type=jnp.float32) for index in range(3)
    ]

    def rotate(part):
        turned = pltpu.roll(part, head // 2, 1)
        return (part * cos_ref[...] + turned * sin_ref[...]).astype(jnp.bfloat16)

    query = rotate(projected[0])
    key_new = rotate(projected[1])
    value_new = projected[2].astype(jnp.bfloat16)
    scale = head ** (-0.5)
    own = jnp.sum(
        query.astype(jnp.float32) * key_new.astype(jnp.float32), axis=1, keepdims=True
    )
    length = length_ref[...]
    peak = own
    for (begin, size), copy in zip(pieces, key_copies):
        copy.wait()
        part = lax.dot_general(
            query,
            keys[begin : begin + size, :],
            (((1,), (1,)), ((), ())),
            preferred_element_type=jnp.float32,
        )
        place = lax.broadcasted_iota(jnp.int32, part.shape, 1)
        mine = place % group == lax.broadcasted_iota(jnp.int32, part.shape, 0)
        inside = place < (length * group - begin)
        part = jnp.where(mine & inside, part, FAR_BELOW)
        scores[:, begin : begin + size] = part
        peak = jnp.maximum(peak, jnp.max(part, axis=1, keepdims=True))

    own_share = jnp.exp((own - peak) * scale)
    denom = own_share
    mixed = own_share * value_new.astype(jnp.float32)
    for (begin, size), copy in zip(pieces, value_copies):
        share = jnp.exp((scores[:, begin : begin + size] - peak) * scale)
        denom = denom + jnp.sum(share, axis=1, keepdims=True)
        copy.wait()
        mixed = mixed + jnp.dot(
            share.astype(jnp.bfloat16),
            values[begin : begin + size, :],
            preferred_element_type=jnp.float32,
        )
    attended = (mixed / denom).astype(jnp.bfloat16)
    part = jnp.dot(attended, out_weight_ref[...], preferred_element_type=jnp.float32)
    for row in range(send_ref.shape[1]):
        send_ref[:, row, :] = part[:, row * LANES : (row + 1) * LANES]


def middle_kernel(received_ref, mixed_ref, width_ref, mix_ref, depth_ref, send_ref, base_ref):
    streams = mixed_ref.shape[0]
    attn_out = jnp.sum(received_ref[...], axis=0)
    state = [mixed_ref[stream] + depth_ref[0, stream] * attn_out for stream in range(streams)]
    combined = sum(width_ref[1, stream] * state[stream] for stream in range(streams))
    normed = normalize(combined)
    half = normed.shape[0] // 2
    ring = lax.axis_size("y")
    step = half // ring
    shift = lax.rem((ring - lax.axis_index("y")) * step, half)
    first = pltpu.roll(normed[:half], shift, 0)
    second = pltpu.roll(normed[half:], shift, 0)
    count = send_ref.shape[0] // 2
    straight = jnp.concatenate([first, second], axis=0).astype(send_ref.dtype)
    crossed = jnp.concatenate([second, first], axis=0).astype(send_ref.dtype)
    shape = (count,) + straight.shape
    send_ref[:count] = jnp.broadcast_to(straight[None], shape)
    send_ref[count:] = jnp.broadcast_to(crossed[None], shape)
    for target in range(streams):
        base_ref[target] = sum(mix_ref[1, stream, target] * state[stream] for stream in range(streams))


def feed_kernel(received_ref, *refs):
    weight_refs, (send_ref, tiles) = refs[:-2], refs[-2:]
    tiles[...] = received_ref[...].astype(jnp.float32)
    part = weight_refs[0].shape[1]
    step = part // LANES
    gate = 0.0
    upward = 0.0
    for index, weight_ref in enumerate(weight_refs):
        piece = jnp.concatenate(
            [tiles[:, index * step + row, :] for row in range(step)], axis=1
        ).astype(jnp.bfloat16)
        gate = gate + jnp.dot(piece, weight_ref[0], preferred_element_type=jnp.float32)
        upward = upward + jnp.dot(piece, weight_ref[1], preferred_element_type=jnp.float32)
    hidden = (gate / (1.0 + jnp.exp(-gate)) * upward).astype(jnp.bfloat16)
    for index, weight_ref in enumerate(weight_refs):
        down = jnp.dot(hidden, weight_ref[2], preferred_element_type=jnp.float32)
        for row in range(step):
            tiles[:, index * step + row, :] = down[:, row * LANES : (row + 1) * LANES]
    send_ref[...] = tiles[...].astype(send_ref.dtype)


def leave_kernel(received_ref, base_ref, depth_ref, out_ref, tiles):
    count = received_ref.shape[0] // 2
    straight = jnp.sum(received_ref[:count].astype(jnp.float32), axis=0)
    crossed = jnp.sum(received_ref[count:].astype(jnp.float32), axis=0)
    half = straight.shape[0] // 2
    step = half // lax.axis_size("y")
    shift = lax.axis_index("y") * step
    first = pltpu.roll(straight[:half] + crossed[half:], shift, 0)
    second = pltpu.roll(straight[half:] + crossed[:half], shift, 0)
    mlp_out = jnp.concatenate([first, second], axis=0)
    for stream in range(tiles.shape[0]):
        tiles[stream] = base_ref[stream] + depth_ref[1, stream] * mlp_out
    for row in range(tiles.shape[1]):
        out_ref[0, :, row * LANES : (row + 1) * LANES] = tiles[:, row, :]


def turn_tables(lengths, head):
    half = head // 2
    index = jnp.arange(half).astype(jnp.float32)
    freqs = jnp.exp(index * (-2.0 * math.log(10000.0) / head))
    angles = lengths.astype(jnp.float32)[:, None] * freqs[None, :]
    cosine = jnp.cos(angles)
    sine = jnp.sin(angles)
    return (
        jnp.concatenate([cosine, cosine], axis=1),
        jnp.concatenate([-sine, sine], axis=1),
    )


def cut(total, size):
    return [(begin, min(size, total - begin)) for begin in range(0, total, size)]


def exchange(rows, axes):
    return lax.all_to_all(rows, axes, split_axis=0, concat_axis=0, tiled=True)


def on_device(
    hyper_state,
    lengths,
    key_cache,
    value_cache,
    attn_in_weight,
    attn_out_weight,
    w_gate,
    w_up,
    w_down,
    width_in,
    stream_mix,
    depth_out,
):
    streams, width = hyper_state.shape[1:]
    group, _, slots, head = key_cache.shape
    blk_count = lax.axis_size("blk")
    ring = lax.axis_size("y")
    plane = ("zlo", "blk")
    plane_count = lax.axis_size(plane)
    tiles = (width // LANES, LANES)
    f32, bf16 = jnp.float32, jnp.bfloat16

    half = w_gate.shape[1] // 2
    piece = jax.ShapeDtypeStruct((3, half, half), bf16)
    own, sent = pl.pallas_call(
        halves_kernel,
        out_shape=[piece, piece],
        in_specs=[HBM] * 3,
        out_specs=[HBM] * 2,
        scratch_shapes=[pltpu.SemaphoreType.DMA((6,))],
        name="halves",
    )(w_gate, w_up, w_down)

    def from_ahead(array, distance):
        return lax.ppermute(
            array, "y", [((place + distance) % ring, place) for place in range(ring)]
        )

    other = lax.ppermute(sent, "zlo", [(0, 1), (1, 0)])
    near = [own] + [from_ahead(own, distance) for distance in range(1, ring)]

    send, mixed = pl.pallas_call(
        enter_kernel,
        out_shape=[
            jax.ShapeDtypeStruct((blk_count,) + tiles, f32),
            jax.ShapeDtypeStruct((streams,) + tiles, f32),
        ],
        in_specs=[VMEM, SMEM, SMEM],
        out_specs=[VMEM] * 2,
        scratch_shapes=[pltpu.VMEM((streams,) + tiles, f32)],
        name="enter",
    )(hyper_state, width_in, stream_mix)
    group_rows = exchange(send, "blk")

    cosine, sine = turn_tables(lengths, head)
    in_cache_order = lambda cache: jnp.transpose(cache[:, 0], (1, 0, 2)).reshape(slots * group, head)
    pieces = cut(slots * group, 4096)
    send = pl.pallas_call(
        functools.partial(attend_kernel, pieces=pieces),
        out_shape=jax.ShapeDtypeStruct((group,) + tiles, f32),
        in_specs=[VMEM] * 5 + [HBM] * 2 + [VMEM],
        out_specs=VMEM,
        scratch_shapes=[
            pltpu.VMEM((slots * group, head), bf16),
            pltpu.VMEM((slots * group, head), bf16),
            pltpu.VMEM((group, slots * group), f32),
            pltpu.SemaphoreType.DMA((len(pieces),)),
            pltpu.SemaphoreType.DMA((len(pieces),)),
        ],
        compiler_params=pltpu.CompilerParams(vmem_limit_bytes=40 * 2**20),
        name="attend",
    )(
        group_rows,
        cosine,
        sine,
        lengths[:, None],
        attn_in_weight,
        in_cache_order(key_cache),
        in_cache_order(value_cache),
        attn_out_weight,
    )
    send, other = lax.optimization_barrier((send, other))
    far = [other] + [from_ahead(other, distance) for distance in range(1, ring)]
    received = exchange(send, "blk")

    send, base = pl.pallas_call(
        middle_kernel,
        out_shape=[
            jax.ShapeDtypeStruct((plane_count,) + tiles, bf16),
            jax.ShapeDtypeStruct((streams,) + tiles, f32),
        ],
        in_specs=[VMEM] * 2 + [SMEM] * 3,
        out_specs=[VMEM] * 2,
        name="middle",
    )(received, mixed, width_in, stream_mix, depth_out)
    received = exchange(send, plane)

    send = pl.pallas_call(
        feed_kernel,
        out_shape=jax.ShapeDtypeStruct((plane_count,) + tiles, bf16),
        in_specs=[VMEM] * (1 + 2 * ring),
        out_specs=VMEM,
        scratch_shapes=[pltpu.VMEM((plane_count,) + tiles, f32)],
        name="feed",
    )(received, *near, *far)
    received = exchange(send, plane)

    return pl.pallas_call(
        leave_kernel,
        out_shape=jax.ShapeDtypeStruct(hyper_state.shape, f32),
        in_specs=[VMEM] * 2 + [SMEM],
        out_specs=VMEM,
        scratch_shapes=[pltpu.VMEM((streams,) + tiles, f32)],
        name="leave",
    )(received, base, depth_out)


def solution(mesh):
    req_count = mesh.shape["req"]
    blk_count = mesh.shape["blk"]
    fine = Mesh(mesh.devices.reshape(2, req_count // 2, blk_count), ("zlo", "y", "blk"))
    req = ("zlo", "y")
    everyone = P(("zlo", "y", "blk"), None, None)
    placed = (
        everyone,
        P(req),
        P(req, "blk", None, None),
        P(req, "blk", None, None),
        P(None, None, "blk"),
        P("blk", None),
        P(req, "blk"),
        P(req, "blk"),
        P("blk", req),
        P(),
        P(),
        P(),
    )
    return jax.shard_map(
        on_device, mesh=fine, in_specs=placed, out_specs=everyone, check_vma=False
    )
```

```python
import functools
import math

import jax
import jax.numpy as jnp
from jax import lax
from jax.experimental import pallas as pl
from jax.experimental.pallas import tpu as pltpu
from jax.sharding import Mesh, PartitionSpec as P

LANES = 128
FAR_BELOW = -1e30
VMEM = pl.BlockSpec(memory_space=pltpu.VMEM)
SMEM = pl.BlockSpec(memory_space=pltpu.SMEM)
HBM = pl.BlockSpec(memory_space=pltpu.HBM)


def normalize(values):
    count = values.shape[0] * values.shape[1]
    center = values - jnp.sum(values, keepdims=True) / count
    spread = jnp.sum(center * center, keepdims=True) / count
    return center * lax.rsqrt(spread + 1e-05)


def enter_kernel(
    state_ref,
    gate_hbm,
    up_hbm,
    down_hbm,
    width_ref,
    mix_ref,
    send_ref,
    mixed_ref,
    own_ref,
    sent_ref,
    tiles,
    sems,
):
    half = own_ref.shape[1]
    side = lax.axis_index("zlo")
    copies = []
    for index, (target, which) in enumerate(((sent_ref, 1 - side), (own_ref, side))):
        begin = pl.multiple_of(which * half, half)
        copies += [
            pltpu.make_async_copy(gate_hbm.at[:, pl.ds(begin, half)], target.at[0], sems.at[3 * index]),
            pltpu.make_async_copy(up_hbm.at[:, pl.ds(begin, half)], target.at[1], sems.at[3 * index + 1]),
            pltpu.make_async_copy(down_hbm.at[pl.ds(begin, half), :], target.at[2], sems.at[3 * index + 2]),
        ]
    for copy in copies:
        copy.start()
    streams, rows = tiles.shape[0], tiles.shape[1]
    for row in range(rows):
        tiles[:, row, :] = state_ref[0, :, row * LANES : (row + 1) * LANES]
    state = [tiles[stream] for stream in range(streams)]
    combined = sum(width_ref[0, stream] * state[stream] for stream in range(streams))
    send_ref[...] = jnp.broadcast_to(normalize(combined)[None], send_ref.shape)
    for target in range(streams):
        mixed_ref[target] = sum(mix_ref[0, stream, target] * state[stream] for stream in range(streams))
    for copy in copies:
        copy.wait()


def turn_tables(lengths):
    head = lengths.shape[1]
    place = lax.broadcasted_iota(jnp.int32, lengths.shape, 1)
    index = (place % (head // 2)).astype(jnp.float32)
    freqs = jnp.exp(index * (-2.0 * math.log(10000.0) / head))
    angles = lengths.astype(jnp.float32) * freqs
    sine = jnp.sin(angles)
    return jnp.cos(angles), jnp.where(place < head // 2, -sine, sine)


def attend_kernel(
    rows_ref,
    length_ref,
    weight_hbm,
    keys_hbm,
    values_hbm,
    out_weight_hbm,
    send_ref,
    weight_ref,
    out_weight_ref,
    keys,
    values,
    scores,
    weight_sems,
    key_sems,
    value_sems,
    *,
    pieces,
):
    def copies(source, target, sems):
        return [
            pltpu.make_async_copy(
                source.at[pl.ds(begin, size)], target.at[pl.ds(begin, size)], sems.at[index]
            )
            for index, (begin, size) in enumerate(pieces)
        ]

    weight_copy = pltpu.make_async_copy(weight_hbm, weight_ref, weight_sems.at[0])
    out_weight_copy = pltpu.make_async_copy(out_weight_hbm, out_weight_ref, weight_sems.at[1])
    key_copies = copies(keys_hbm, keys, key_sems)
    value_copies = copies(values_hbm, values, value_sems)
    for copy in [weight_copy] + key_copies + value_copies + [out_weight_copy]:
        copy.start()

    group = rows_ref.shape[0]
    head = keys.shape[1]
    request = lax.broadcasted_iota(jnp.int32, (group, head), 0)
    lengths = jnp.zeros((group, head), jnp.int32)
    for row in range(group):
        lengths = jnp.where(request == row, length_ref[row], lengths)
    cosine, sine = turn_tables(lengths)
    rows = jnp.concatenate([rows_ref[:, row, :] for row in range(rows_ref.shape[1])], axis=1)
    rows = rows.astype(jnp.bfloat16)
    weight_copy.wait()
    projected = [
        jnp.dot(rows, weight_ref[index], preferred_element_type=jnp.float32) for index in range(3)
    ]

    def rotate(part):
        turned = pltpu.roll(part, head // 2, 1)
        return (part * cosine + turned * sine).astype(jnp.bfloat16)

    query = rotate(projected[0])
    key_new = rotate(projected[1])
    value_new = projected[2].astype(jnp.bfloat16)
    scale = head ** (-0.5)
    own = jnp.sum(
        query.astype(jnp.float32) * key_new.astype(jnp.float32), axis=1, keepdims=True
    )
    length = lengths[:, :1]
    peak = own
    for (begin, size), copy in zip(pieces, key_copies):
        copy.wait()
        part = lax.dot_general(
            query,
            keys[begin : begin + size, :],
            (((1,), (1,)), ((), ())),
            preferred_element_type=jnp.float32,
        )
        place = lax.broadcasted_iota(jnp.int32, part.shape, 1)
        mine = place % group == lax.broadcasted_iota(jnp.int32, part.shape, 0)
        inside = place < (length * group - begin)
        part = jnp.where(mine & inside, part, FAR_BELOW)
        scores[:, begin : begin + size] = part
        peak = jnp.maximum(peak, jnp.max(part, axis=1, keepdims=True))

    own_share = jnp.exp((own - peak) * scale)
    denom = own_share
    mixed = own_share * value_new.astype(jnp.float32)
    for (begin, size), copy in zip(pieces, value_copies):
        share = jnp.exp((scores[:, begin : begin + size] - peak) * scale)
        denom = denom + jnp.sum(share, axis=1, keepdims=True)
        copy.wait()
        mixed = mixed + jnp.dot(
            share.astype(jnp.bfloat16),
            values[begin : begin + size, :],
            preferred_element_type=jnp.float32,
        )
    attended = (mixed / denom).astype(jnp.bfloat16)
    out_weight_copy.wait()
    part = jnp.dot(attended, out_weight_ref[...], preferred_element_type=jnp.float32)
    for row in range(send_ref.shape[1]):
        send_ref[:, row, :] = part[:, row * LANES : (row + 1) * LANES]


def middle_kernel(received_ref, mixed_ref, width_ref, mix_ref, depth_ref, send_ref, base_ref):
    streams = mixed_ref.shape[0]
    attn_out = jnp.sum(received_ref[...], axis=0)
    state = [mixed_ref[stream] + depth_ref[0, stream] * attn_out for stream in range(streams)]
    combined = sum(width_ref[1, stream] * state[stream] for stream in range(streams))
    normed = normalize(combined)
    half = normed.shape[0] // 2
    ring = lax.axis_size("y")
    shift = lax.rem((ring - lax.axis_index("y")) * (half // ring), half)
    first = pltpu.roll(normed[:half], shift, 0)
    second = pltpu.roll(normed[half:], shift, 0)
    count = send_ref.shape[0] // 2
    straight = jnp.concatenate([first, second], axis=0).astype(send_ref.dtype)
    crossed = jnp.concatenate([second, first], axis=0).astype(send_ref.dtype)
    shape = (count,) + straight.shape
    send_ref[:count] = jnp.broadcast_to(straight[None], shape)
    send_ref[count:] = jnp.broadcast_to(crossed[None], shape)
    for target in range(streams):
        base_ref[target] = sum(mix_ref[1, stream, target] * state[stream] for stream in range(streams))


def feed_kernel(received_ref, *refs):
    weight_hbms, (send_ref, weights, tiles, sems) = refs[:-4], refs[-4:]
    ring = len(weight_hbms)
    copies = [
        pltpu.make_async_copy(weight_hbms[index], weights.at[index], sems.at[index])
        for index in range(ring)
    ]
    for copy in copies:
        copy.start()
    tiles[...] = received_ref[...].astype(jnp.float32)
    step = weights.shape[3] // LANES
    order = [(index, side) for index in range(ring) for side in range(2)]
    gate = 0.0
    upward = 0.0
    for index, side in order:
        begin = (side * ring + index) * step
        piece = jnp.concatenate(
            [tiles[:, begin + row, :] for row in range(step)], axis=1
        ).astype(jnp.bfloat16)
        if side == 0:
            copies[index].wait()
        gate = gate + jnp.dot(piece, weights[index, side, 0], preferred_element_type=jnp.float32)
        upward = upward + jnp.dot(piece, weights[index, side, 1], preferred_element_type=jnp.float32)
    hidden = (gate / (1.0 + jnp.exp(-gate)) * upward).astype(jnp.bfloat16)
    for index, side in order:
        begin = (side * ring + index) * step
        down = jnp.dot(hidden, weights[index, side, 2], preferred_element_type=jnp.float32)
        for row in range(step):
            tiles[:, begin + row, :] = down[:, row * LANES : (row + 1) * LANES]
    send_ref[...] = tiles[...].astype(send_ref.dtype)


def leave_kernel(received_ref, base_ref, depth_ref, out_ref, tiles):
    count = received_ref.shape[0] // 2
    straight = jnp.sum(received_ref[:count].astype(jnp.float32), axis=0)
    crossed = jnp.sum(received_ref[count:].astype(jnp.float32), axis=0)
    half = straight.shape[0] // 2
    step = half // lax.axis_size("y")
    shift = lax.axis_index("y") * step
    first = pltpu.roll(straight[:half] + crossed[half:], shift, 0)
    second = pltpu.roll(straight[half:] + crossed[:half], shift, 0)
    mlp_out = jnp.concatenate([first, second], axis=0)
    for stream in range(tiles.shape[0]):
        tiles[stream] = base_ref[stream] + depth_ref[1, stream] * mlp_out
    for row in range(tiles.shape[1]):
        out_ref[0, :, row * LANES : (row + 1) * LANES] = tiles[:, row, :]


def cut(total, size):
    return [(begin, min(size, total - begin)) for begin in range(0, total, size)]


def exchange(rows, axes):
    return lax.all_to_all(rows, axes, split_axis=0, concat_axis=0, tiled=True)


def on_device(
    hyper_state,
    lengths,
    key_cache,
    value_cache,
    attn_in_weight,
    attn_out_weight,
    w_gate,
    w_up,
    w_down,
    width_in,
    stream_mix,
    depth_out,
):
    streams, width = hyper_state.shape[1:]
    group, _, slots, head = key_cache.shape
    blk_count = lax.axis_size("blk")
    ring = lax.axis_size("y")
    plane = ("zlo", "blk")
    plane_count = lax.axis_size(plane)
    tiles = (width // LANES, LANES)
    f32, bf16 = jnp.float32, jnp.bfloat16

    half = w_gate.shape[1] // 2
    piece = jax.ShapeDtypeStruct((3, half, half), bf16)
    send, mixed, own, sent = pl.pallas_call(
        enter_kernel,
        out_shape=[
            jax.ShapeDtypeStruct((blk_count,) + tiles, f32),
            jax.ShapeDtypeStruct((streams,) + tiles, f32),
            piece,
            piece,
        ],
        in_specs=[VMEM] + [HBM] * 3 + [SMEM] * 2,
        out_specs=[VMEM] * 4,
        scratch_shapes=[pltpu.VMEM((streams,) + tiles, f32), pltpu.SemaphoreType.DMA((6,))],
        name="enter",
    )(hyper_state, w_gate, w_up, w_down, width_in, stream_mix)

    other = lax.ppermute(sent, "zlo", [(0, 1), (1, 0)])
    both = jnp.stack([own, other])
    weights = [both] + [
        lax.ppermute(both, "y", [((place + distance) % ring, place) for place in range(ring)])
        for distance in range(1, ring)
    ]
    group_rows = exchange(send, "blk")

    in_cache_order = lambda cache: jnp.transpose(cache[:, 0], (1, 0, 2)).reshape(slots * group, head)
    pieces = cut(slots * group, 8192)
    send = pl.pallas_call(
        functools.partial(attend_kernel, pieces=pieces),
        out_shape=jax.ShapeDtypeStruct((group,) + tiles, f32),
        in_specs=[VMEM, SMEM] + [HBM] * 4,
        out_specs=VMEM,
        scratch_shapes=[
            pltpu.VMEM(attn_in_weight.shape, bf16),
            pltpu.VMEM(attn_out_weight.shape, bf16),
            pltpu.VMEM((slots * group, head), bf16),
            pltpu.VMEM((slots * group, head), bf16),
            pltpu.VMEM((group, slots * group), f32),
            pltpu.SemaphoreType.DMA((2,)),
            pltpu.SemaphoreType.DMA((len(pieces),)),
            pltpu.SemaphoreType.DMA((len(pieces),)),
        ],
        compiler_params=pltpu.CompilerParams(vmem_limit_bytes=63 * 2**20),
        cost_estimate=pl.CostEstimate(flops=3 * 10**12, transcendentals=0, bytes_accessed=20 * 2**20),
        name="attend",
    )(
        group_rows,
        lengths,
        attn_in_weight,
        in_cache_order(key_cache),
        in_cache_order(value_cache),
        attn_out_weight,
    )
    received = exchange(send, "blk")

    send, base = pl.pallas_call(
        middle_kernel,
        out_shape=[
            jax.ShapeDtypeStruct((plane_count,) + tiles, bf16),
            jax.ShapeDtypeStruct((streams,) + tiles, f32),
        ],
        in_specs=[VMEM] * 2 + [SMEM] * 3,
        out_specs=[VMEM] * 2,
        name="middle",
    )(received, mixed, width_in, stream_mix, depth_out)
    received = exchange(send, plane)

    send = pl.pallas_call(
        feed_kernel,
        out_shape=jax.ShapeDtypeStruct((plane_count,) + tiles, bf16),
        in_specs=[VMEM] + [HBM] * ring,
        out_specs=VMEM,
        scratch_shapes=[
            pltpu.VMEM((ring,) + both.shape, bf16),
            pltpu.VMEM((plane_count,) + tiles, f32),
            pltpu.SemaphoreType.DMA((ring,)),
        ],
        name="feed",
    )(received, *weights)
    received = exchange(send, plane)

    return pl.pallas_call(
        leave_kernel,
        out_shape=jax.ShapeDtypeStruct(hyper_state.shape, f32),
        in_specs=[VMEM] * 2 + [SMEM],
        out_specs=VMEM,
        scratch_shapes=[pltpu.VMEM((streams,) + tiles, f32)],
        name="leave",
    )(received, base, depth_out)


def solution(mesh):
    req_count = mesh.shape["req"]
    blk_count = mesh.shape["blk"]
    fine = Mesh(mesh.devices.reshape(2, req_count // 2, blk_count), ("zlo", "y", "blk"))
    req = ("zlo", "y")
    everyone = P(("zlo", "y", "blk"), None, None)
    placed = (
        everyone,
        P(req),
        P(req, "blk", None, None),
        P(req, "blk", None, None),
        P(None, None, "blk"),
        P("blk", None),
        P(req, "blk"),
        P(req, "blk"),
        P("blk", req),
        P(),
        P(),
        P(),
    )
    return jax.shard_map(
        on_device, mesh=fine, in_specs=placed, out_specs=everyone, check_vma=False
    )
```

```python
import functools
import math

import jax
import jax.numpy as jnp
from jax import lax
from jax.experimental import pallas as pl
from jax.experimental.pallas import tpu as pltpu
from jax.sharding import Mesh, PartitionSpec as P

LANES = 128
FAR_BELOW = -1e30
DEPTH = 12
VMEM = pl.BlockSpec(memory_space=pltpu.VMEM)
SMEM = pl.BlockSpec(memory_space=pltpu.SMEM)
HBM = pl.BlockSpec(memory_space=pltpu.HBM)


def normalize(values):
    count = values.shape[0] * values.shape[1]
    center = values - jnp.sum(values, keepdims=True) / count
    spread = jnp.sum(center * center, keepdims=True) / count
    return center * lax.rsqrt(spread + 1e-05)


def enter_kernel(
    state_ref,
    gate_hbm,
    up_hbm,
    down_hbm,
    width_ref,
    mix_ref,
    send_ref,
    mixed_ref,
    own_ref,
    sent_ref,
    tiles,
    sems,
):
    half = own_ref.shape[1]
    side = lax.axis_index("zlo")
    copies = []
    for index, (target, which) in enumerate(((sent_ref, 1 - side), (own_ref, side))):
        begin = pl.multiple_of(which * half, half)
        copies += [
            pltpu.make_async_copy(gate_hbm.at[:, pl.ds(begin, half)], target.at[0], sems.at[3 * index]),
            pltpu.make_async_copy(up_hbm.at[:, pl.ds(begin, half)], target.at[1], sems.at[3 * index + 1]),
            pltpu.make_async_copy(down_hbm.at[pl.ds(begin, half), :], target.at[2], sems.at[3 * index + 2]),
        ]
    for copy in copies:
        copy.start()
    streams, rows = tiles.shape[0], tiles.shape[1]
    for row in range(rows):
        tiles[:, row, :] = state_ref[0, :, row * LANES : (row + 1) * LANES]
    state = [tiles[stream] for stream in range(streams)]
    combined = sum(width_ref[0, stream] * state[stream] for stream in range(streams))
    send_ref[...] = jnp.broadcast_to(normalize(combined)[None], send_ref.shape)
    for target in range(streams):
        mixed_ref[target] = sum(mix_ref[0, stream, target] * state[stream] for stream in range(streams))
    for copy in copies:
        copy.wait()


def turn_tables(lengths):
    head = lengths.shape[1]
    place = lax.broadcasted_iota(jnp.int32, lengths.shape, 1)
    index = (place % (head // 2)).astype(jnp.float32)
    freqs = jnp.exp(index * (-2.0 * math.log(10000.0) / head))
    angles = lengths.astype(jnp.float32) * freqs
    sine = jnp.sin(angles)
    return jnp.cos(angles), jnp.where(place < head // 2, -sine, sine)


def attend_kernel(
    rows_ref,
    length_ref,
    weight_hbm,
    keys_hbm,
    values_hbm,
    out_weight_hbm,
    send_ref,
    weight_ref,
    out_weight_ref,
    keys,
    values,
    scores,
    sems,
    *,
    pieces,
    steps,
):
    queue = [pltpu.make_async_copy(weight_hbm, weight_ref, sems.at[0])]
    for source, target in ((keys_hbm, keys), (values_hbm, values)):
        for begin, size in pieces:
            queue.append(
                pltpu.make_async_copy(
                    source.at[pl.ds(begin, size)],
                    target.at[pl.ds(begin, size)],
                    sems.at[len(queue)],
                )
            )
    queue.append(pltpu.make_async_copy(out_weight_hbm, out_weight_ref, sems.at[len(queue)]))
    waited = iter(range(len(queue)))

    def arrive():
        index = next(waited)
        queue[index].wait()
        if index + DEPTH < len(queue):
            queue[index + DEPTH].start()

    for copy in queue[:DEPTH]:
        copy.start()

    group = rows_ref.shape[0]
    head = keys.shape[1]
    request = lax.broadcasted_iota(jnp.int32, (group, head), 0)
    lengths = jnp.zeros((group, head), jnp.int32)
    for row in range(group):
        lengths = jnp.where(request == row, length_ref[row], lengths)
    cosine, sine = turn_tables(lengths)
    rows = jnp.concatenate([rows_ref[:, row, :] for row in range(rows_ref.shape[1])], axis=1)
    rows = rows.astype(jnp.bfloat16)
    arrive()
    projected = [
        jnp.dot(rows, weight_ref[index], preferred_element_type=jnp.float32) for index in range(3)
    ]

    def rotate(part):
        turned = pltpu.roll(part, head // 2, 1)
        return (part * cosine + turned * sine).astype(jnp.bfloat16)

    query = rotate(projected[0])
    key_new = rotate(projected[1])
    value_new = projected[2].astype(jnp.bfloat16)
    scale = head ** (-0.5)
    own = jnp.sum(
        query.astype(jnp.float32) * key_new.astype(jnp.float32), axis=1, keepdims=True
    )
    length = lengths[:, :1]
    peak = own

    def within(begin, size):
        return [piece for piece in pieces if begin <= piece[0] < begin + size]

    for begin, size in steps:
        for _ in within(begin, size):
            arrive()
        part = lax.dot_general(
            query,
            keys[begin : begin + size, :],
            (((1,), (1,)), ((), ())),
            preferred_element_type=jnp.float32,
        )
        place = lax.broadcasted_iota(jnp.int32, part.shape, 1)
        mine = place % group == lax.broadcasted_iota(jnp.int32, part.shape, 0)
        inside = place < (length * group - begin)
        part = jnp.where(mine & inside, part, FAR_BELOW)
        scores[:, begin : begin + size] = part
        peak = jnp.maximum(peak, jnp.max(part, axis=1, keepdims=True))

    own_share = jnp.exp((own - peak) * scale)
    denom = own_share
    mixed = own_share * value_new.astype(jnp.float32)
    for begin, size in steps:
        share = jnp.exp((scores[:, begin : begin + size] - peak) * scale)
        denom = denom + jnp.sum(share, axis=1, keepdims=True)
        for _ in within(begin, size):
            arrive()
        mixed = mixed + jnp.dot(
            share.astype(jnp.bfloat16),
            values[begin : begin + size, :],
            preferred_element_type=jnp.float32,
        )
    attended = (mixed / denom).astype(jnp.bfloat16)
    arrive()
    part = jnp.dot(attended, out_weight_ref[...], preferred_element_type=jnp.float32)
    for row in range(send_ref.shape[1]):
        send_ref[:, row, :] = part[:, row * LANES : (row + 1) * LANES]


def middle_kernel(received_ref, mixed_ref, width_ref, mix_ref, depth_ref, send_ref, base_ref):
    streams = mixed_ref.shape[0]
    attn_out = jnp.sum(received_ref[...], axis=0)
    state = [mixed_ref[stream] + depth_ref[0, stream] * attn_out for stream in range(streams)]
    combined = sum(width_ref[1, stream] * state[stream] for stream in range(streams))
    normed = normalize(combined)
    half = normed.shape[0] // 2
    ring = lax.axis_size("y")
    shift = lax.rem((ring - lax.axis_index("y")) * (half // ring), half)
    first = pltpu.roll(normed[:half], shift, 0)
    second = pltpu.roll(normed[half:], shift, 0)
    count = send_ref.shape[0] // 2
    straight = jnp.concatenate([first, second], axis=0).astype(send_ref.dtype)
    crossed = jnp.concatenate([second, first], axis=0).astype(send_ref.dtype)
    shape = (count,) + straight.shape
    send_ref[:count] = jnp.broadcast_to(straight[None], shape)
    send_ref[count:] = jnp.broadcast_to(crossed[None], shape)
    for target in range(streams):
        base_ref[target] = sum(mix_ref[1, stream, target] * state[stream] for stream in range(streams))


def feed_kernel(received_ref, *refs):
    weight_hbms, (send_ref, weights, tiles, sems) = refs[:-4], refs[-4:]
    copies = [
        pltpu.make_async_copy(source, weights.at[index], sems.at[index])
        for index, source in enumerate(weight_hbms)
    ]
    for copy in copies:
        copy.start()
    tiles[...] = received_ref[...].astype(jnp.float32)
    step = weights.shape[2] // LANES
    gate = 0.0
    upward = 0.0
    for index, copy in enumerate(copies):
        piece = jnp.concatenate(
            [tiles[:, index * step + row, :] for row in range(step)], axis=1
        ).astype(jnp.bfloat16)
        copy.wait()
        gate = gate + jnp.dot(piece, weights[index, 0], preferred_element_type=jnp.float32)
        upward = upward + jnp.dot(piece, weights[index, 1], preferred_element_type=jnp.float32)
    hidden = (gate / (1.0 + jnp.exp(-gate)) * upward).astype(jnp.bfloat16)
    for index in range(len(copies)):
        down = jnp.dot(hidden, weights[index, 2], preferred_element_type=jnp.float32)
        for row in range(step):
            tiles[:, index * step + row, :] = down[:, row * LANES : (row + 1) * LANES]
    send_ref[...] = tiles[...].astype(send_ref.dtype)


def leave_kernel(received_ref, base_ref, depth_ref, out_ref, tiles):
    count = received_ref.shape[0] // 2
    straight = jnp.sum(received_ref[:count].astype(jnp.float32), axis=0)
    crossed = jnp.sum(received_ref[count:].astype(jnp.float32), axis=0)
    half = straight.shape[0] // 2
    step = half // lax.axis_size("y")
    shift = lax.axis_index("y") * step
    first = pltpu.roll(straight[:half] + crossed[half:], shift, 0)
    second = pltpu.roll(straight[half:] + crossed[:half], shift, 0)
    mlp_out = jnp.concatenate([first, second], axis=0)
    for stream in range(tiles.shape[0]):
        tiles[stream] = base_ref[stream] + depth_ref[1, stream] * mlp_out
    for row in range(tiles.shape[1]):
        out_ref[0, :, row * LANES : (row + 1) * LANES] = tiles[:, row, :]


def cut(total, size):
    return [(begin, min(size, total - begin)) for begin in range(0, total, size)]


def exchange(rows, axes):
    return lax.all_to_all(rows, axes, split_axis=0, concat_axis=0, tiled=True)


def on_device(
    hyper_state,
    lengths,
    key_cache,
    value_cache,
    attn_in_weight,
    attn_out_weight,
    w_gate,
    w_up,
    w_down,
    width_in,
    stream_mix,
    depth_out,
):
    streams, width = hyper_state.shape[1:]
    group, _, slots, head = key_cache.shape
    blk_count = lax.axis_size("blk")
    ring = lax.axis_size("y")
    plane = ("zlo", "blk")
    plane_count = lax.axis_size(plane)
    tiles = (width // LANES, LANES)
    f32, bf16 = jnp.float32, jnp.bfloat16

    half = w_gate.shape[1] // 2
    piece = jax.ShapeDtypeStruct((3, half, half), bf16)
    send, mixed, own, sent = pl.pallas_call(
        enter_kernel,
        out_shape=[
            jax.ShapeDtypeStruct((blk_count,) + tiles, f32),
            jax.ShapeDtypeStruct((streams,) + tiles, f32),
            piece,
            piece,
        ],
        in_specs=[VMEM] + [HBM] * 3 + [SMEM] * 2,
        out_specs=[VMEM] * 4,
        scratch_shapes=[pltpu.VMEM((streams,) + tiles, f32), pltpu.SemaphoreType.DMA((6,))],
        name="enter",
    )(hyper_state, w_gate, w_up, w_down, width_in, stream_mix)

    def gathered(array):
        return [array] + [
            lax.ppermute(array, "y", [((place + distance) % ring, place) for place in range(ring)])
            for distance in range(1, ring)
        ]

    near = gathered(own)
    far = gathered(lax.ppermute(sent, "zlo", [(0, 1), (1, 0)]))
    group_rows = exchange(send, "blk")

    in_cache_order = lambda cache: jnp.transpose(cache[:, 0], (1, 0, 2)).reshape(slots * group, head)
    pieces = cut(slots * group, 4096)
    steps = cut(slots * group, 8192)
    send = pl.pallas_call(
        functools.partial(attend_kernel, pieces=pieces, steps=steps),
        out_shape=jax.ShapeDtypeStruct((group,) + tiles, f32),
        in_specs=[VMEM, SMEM] + [HBM] * 4,
        out_specs=VMEM,
        scratch_shapes=[
            pltpu.VMEM(attn_in_weight.shape, bf16),
            pltpu.VMEM(attn_out_weight.shape, bf16),
            pltpu.VMEM((slots * group, head), bf16),
            pltpu.VMEM((slots * group, head), bf16),
            pltpu.VMEM((group, slots * group), f32),
            pltpu.SemaphoreType.DMA((2 + 2 * len(pieces),)),
        ],
        compiler_params=pltpu.CompilerParams(vmem_limit_bytes=63 * 2**20),
        cost_estimate=pl.CostEstimate(flops=3 * 10**12, transcendentals=0, bytes_accessed=20 * 2**20),
        name="attend",
    )(
        group_rows,
        lengths,
        attn_in_weight,
        in_cache_order(key_cache),
        in_cache_order(value_cache),
        attn_out_weight,
    )
    received = exchange(send, "blk")
    received, near = lax.optimization_barrier((received, near))

    send, base = pl.pallas_call(
        middle_kernel,
        out_shape=[
            jax.ShapeDtypeStruct((plane_count,) + tiles, bf16),
            jax.ShapeDtypeStruct((streams,) + tiles, f32),
        ],
        in_specs=[VMEM] * 2 + [SMEM] * 3,
        out_specs=[VMEM] * 2,
        cost_estimate=pl.CostEstimate(flops=2 * 10**9, transcendentals=0, bytes_accessed=2**20),
        name="middle",
    )(received, mixed, width_in, stream_mix, depth_out)
    received = exchange(send, plane)

    send = pl.pallas_call(
        feed_kernel,
        out_shape=jax.ShapeDtypeStruct((plane_count,) + tiles, bf16),
        in_specs=[VMEM] + [HBM] * (2 * ring),
        out_specs=VMEM,
        scratch_shapes=[
            pltpu.VMEM((2 * ring,) + own.shape, bf16),
            pltpu.VMEM((plane_count,) + tiles, f32),
            pltpu.SemaphoreType.DMA((2 * ring,)),
        ],
        name="feed",
    )(received, *near, *far)
    received = exchange(send, plane)

    return pl.pallas_call(
        leave_kernel,
        out_shape=jax.ShapeDtypeStruct(hyper_state.shape, f32),
        in_specs=[VMEM] * 2 + [SMEM],
        out_specs=VMEM,
        scratch_shapes=[pltpu.VMEM((streams,) + tiles, f32)],
        name="leave",
    )(received, base, depth_out)


def solution(mesh):
    req_count = mesh.shape["req"]
    blk_count = mesh.shape["blk"]
    fine = Mesh(mesh.devices.reshape(2, req_count // 2, blk_count), ("zlo", "y", "blk"))
    req = ("zlo", "y")
    everyone = P(("zlo", "y", "blk"), None, None)
    placed = (
        everyone,
        P(req),
        P(req, "blk", None, None),
        P(req, "blk", None, None),
        P(None, None, "blk"),
        P("blk", None),
        P(req, "blk"),
        P(req, "blk"),
        P("blk", req),
        P(),
        P(),
        P(),
    )
    return jax.shard_map(
        on_device, mesh=fine, in_specs=placed, out_specs=everyone, check_vma=False
    )
```

```python
import functools
import math

import jax
import jax.numpy as jnp
from jax import lax
from jax.experimental import pallas as pl
from jax.experimental.pallas import tpu as pltpu
from jax.sharding import Mesh, PartitionSpec as P

LANES = 128
FAR_BELOW = -1e30
DEPTH = 12
VMEM = pl.BlockSpec(memory_space=pltpu.VMEM)
SMEM = pl.BlockSpec(memory_space=pltpu.SMEM)
HBM = pl.BlockSpec(memory_space=pltpu.HBM)


def normalize(values):
    count = values.shape[0] * values.shape[1]
    center = values - jnp.sum(values, keepdims=True) / count
    spread = jnp.sum(center * center, keepdims=True) / count
    return center * lax.rsqrt(spread + 1e-05)


def enter_kernel(
    state_ref,
    gate_hbm,
    up_hbm,
    down_hbm,
    width_ref,
    mix_ref,
    send_ref,
    mixed_ref,
    own_ref,
    sent_ref,
    tiles,
    sems,
):
    half = own_ref.shape[1]
    side = lax.axis_index("zlo")
    copies = []
    for index, (target, which) in enumerate(((sent_ref, 1 - side), (own_ref, side))):
        begin = pl.multiple_of(which * half, half)
        copies += [
            pltpu.make_async_copy(gate_hbm.at[:, pl.ds(begin, half)], target.at[0], sems.at[3 * index]),
            pltpu.make_async_copy(up_hbm.at[:, pl.ds(begin, half)], target.at[1], sems.at[3 * index + 1]),
            pltpu.make_async_copy(down_hbm.at[pl.ds(begin, half), :], target.at[2], sems.at[3 * index + 2]),
        ]
    for copy in copies:
        copy.start()
    streams, rows = tiles.shape[0], tiles.shape[1]
    for row in range(rows):
        tiles[:, row, :] = state_ref[0, :, row * LANES : (row + 1) * LANES]
    state = [tiles[stream] for stream in range(streams)]
    combined = sum(width_ref[0, stream] * state[stream] for stream in range(streams))
    send_ref[...] = jnp.broadcast_to(normalize(combined)[None], send_ref.shape)
    for target in range(streams):
        mixed_ref[target] = sum(mix_ref[0, stream, target] * state[stream] for stream in range(streams))
    for copy in copies:
        copy.wait()


def turn_tables(lengths):
    head = lengths.shape[1]
    place = lax.broadcasted_iota(jnp.int32, lengths.shape, 1)
    index = (place % (head // 2)).astype(jnp.float32)
    freqs = jnp.exp(index * (-2.0 * math.log(10000.0) / head))
    angles = lengths.astype(jnp.float32) * freqs
    sine = jnp.sin(angles)
    return jnp.cos(angles), jnp.where(place < head // 2, -sine, sine)


def attend_kernel(
    rows_ref,
    length_ref,
    weight_hbm,
    keys_hbm,
    values_hbm,
    out_weight_hbm,
    send_ref,
    weight_ref,
    out_weight_ref,
    keys,
    values,
    scores,
    sems,
    *,
    pieces,
    steps,
):
    queue = [pltpu.make_async_copy(weight_hbm, weight_ref, sems.at[0])]
    for source, target in ((keys_hbm, keys), (values_hbm, values)):
        for begin, size in pieces:
            queue.append(
                pltpu.make_async_copy(
                    source.at[pl.ds(begin, size)],
                    target.at[pl.ds(begin, size)],
                    sems.at[len(queue)],
                )
            )
    queue.append(pltpu.make_async_copy(out_weight_hbm, out_weight_ref, sems.at[len(queue)]))
    waited = iter(range(len(queue)))

    def arrive():
        index = next(waited)
        queue[index].wait()
        if index + DEPTH < len(queue):
            queue[index + DEPTH].start()

    for copy in queue[:DEPTH]:
        copy.start()

    group = rows_ref.shape[0]
    head = keys.shape[1]
    request = lax.broadcasted_iota(jnp.int32, (group, head), 0)
    lengths = jnp.zeros((group, head), jnp.int32)
    for row in range(group):
        lengths = jnp.where(request == row, length_ref[row], lengths)
    cosine, sine = turn_tables(lengths)
    rows = jnp.concatenate([rows_ref[:, row, :] for row in range(rows_ref.shape[1])], axis=1)
    rows = rows.astype(jnp.bfloat16)
    arrive()
    projected = [
        jnp.dot(rows, weight_ref[index], preferred_element_type=jnp.float32) for index in range(3)
    ]

    def rotate(part):
        turned = pltpu.roll(part, head // 2, 1)
        return (part * cosine + turned * sine).astype(jnp.bfloat16)

    query = rotate(projected[0])
    key_new = rotate(projected[1])
    value_new = projected[2].astype(jnp.bfloat16)
    scale = head ** (-0.5)
    own = jnp.sum(
        query.astype(jnp.float32) * key_new.astype(jnp.float32), axis=1, keepdims=True
    )
    length = lengths[:, :1]
    peak = own

    def within(begin, size):
        return [piece for piece in pieces if begin <= piece[0] < begin + size]

    for begin, size in steps:
        for _ in within(begin, size):
            arrive()
        part = lax.dot_general(
            query,
            keys[begin : begin + size, :],
            (((1,), (1,)), ((), ())),
            preferred_element_type=jnp.float32,
        )
        place = lax.broadcasted_iota(jnp.int32, part.shape, 1)
        mine = place % group == lax.broadcasted_iota(jnp.int32, part.shape, 0)
        inside = place < (length * group - begin)
        part = jnp.where(mine & inside, part, FAR_BELOW)
        scores[:, begin : begin + size] = part
        peak = jnp.maximum(peak, jnp.max(part, axis=1, keepdims=True))

    own_share = jnp.exp((own - peak) * scale)
    denom = own_share
    mixed = own_share * value_new.astype(jnp.float32)
    for begin, size in steps:
        share = jnp.exp((scores[:, begin : begin + size] - peak) * scale)
        denom = denom + jnp.sum(share, axis=1, keepdims=True)
        for _ in within(begin, size):
            arrive()
        mixed = mixed + jnp.dot(
            share.astype(jnp.bfloat16),
            values[begin : begin + size, :],
            preferred_element_type=jnp.float32,
        )
    attended = (mixed / denom).astype(jnp.bfloat16)
    arrive()
    part = jnp.dot(attended, out_weight_ref[...], preferred_element_type=jnp.float32)
    for row in range(send_ref.shape[1]):
        send_ref[:, row, :] = part[:, row * LANES : (row + 1) * LANES]


def middle_kernel(received_ref, mixed_ref, width_ref, mix_ref, depth_ref, send_ref, base_ref):
    streams = mixed_ref.shape[0]
    attn_out = jnp.sum(received_ref[...], axis=0)
    state = [mixed_ref[stream] + depth_ref[0, stream] * attn_out for stream in range(streams)]
    combined = sum(width_ref[1, stream] * state[stream] for stream in range(streams))
    normed = normalize(combined)
    half = normed.shape[0] // 2
    ring = lax.axis_size("y")
    shift = lax.rem((ring - lax.axis_index("y")) * (half // ring), half)
    first = pltpu.roll(normed[:half], shift, 0)
    second = pltpu.roll(normed[half:], shift, 0)
    count = send_ref.shape[0] // 2
    straight = jnp.concatenate([first, second], axis=0).astype(send_ref.dtype)
    crossed = jnp.concatenate([second, first], axis=0).astype(send_ref.dtype)
    shape = (count,) + straight.shape
    send_ref[:count] = jnp.broadcast_to(straight[None], shape)
    send_ref[count:] = jnp.broadcast_to(crossed[None], shape)
    for target in range(streams):
        base_ref[target] = sum(mix_ref[1, stream, target] * state[stream] for stream in range(streams))


def feed_kernel(received_ref, *refs):
    weight_hbms, (send_ref, weights, tiles, sems) = refs[:-4], refs[-4:]
    copies = [
        pltpu.make_async_copy(source, weights.at[index], sems.at[index])
        for index, source in enumerate(weight_hbms)
    ]
    for copy in copies:
        copy.start()
    tiles[...] = received_ref[...].astype(jnp.float32)
    step = weights.shape[2] // LANES
    gate = 0.0
    upward = 0.0
    for index, copy in enumerate(copies):
        piece = jnp.concatenate(
            [tiles[:, index * step + row, :] for row in range(step)], axis=1
        ).astype(jnp.bfloat16)
        copy.wait()
        gate = gate + jnp.dot(piece, weights[index, 0], preferred_element_type=jnp.float32)
        upward = upward + jnp.dot(piece, weights[index, 1], preferred_element_type=jnp.float32)
    hidden = (gate / (1.0 + jnp.exp(-gate)) * upward).astype(jnp.bfloat16)
    for index in range(len(copies)):
        down = jnp.dot(hidden, weights[index, 2], preferred_element_type=jnp.float32)
        for row in range(step):
            tiles[:, index * step + row, :] = down[:, row * LANES : (row + 1) * LANES]
    send_ref[...] = tiles[...].astype(send_ref.dtype)


def leave_kernel(received_ref, base_ref, depth_ref, out_ref, tiles):
    count = received_ref.shape[0] // 2
    straight = jnp.sum(received_ref[:count].astype(jnp.float32), axis=0)
    crossed = jnp.sum(received_ref[count:].astype(jnp.float32), axis=0)
    half = straight.shape[0] // 2
    step = half // lax.axis_size("y")
    shift = lax.axis_index("y") * step
    first = pltpu.roll(straight[:half] + crossed[half:], shift, 0)
    second = pltpu.roll(straight[half:] + crossed[:half], shift, 0)
    mlp_out = jnp.concatenate([first, second], axis=0)
    for stream in range(tiles.shape[0]):
        tiles[stream] = base_ref[stream] + depth_ref[1, stream] * mlp_out
    for row in range(tiles.shape[1]):
        out_ref[0, :, row * LANES : (row + 1) * LANES] = tiles[:, row, :]


def cut(total, size):
    return [(begin, min(size, total - begin)) for begin in range(0, total, size)]


def exchange(rows, axes):
    return lax.all_to_all(rows, axes, split_axis=0, concat_axis=0, tiled=True)


def on_device(
    hyper_state,
    lengths,
    key_cache,
    value_cache,
    attn_in_weight,
    attn_out_weight,
    w_gate,
    w_up,
    w_down,
    width_in,
    stream_mix,
    depth_out,
):
    streams, width = hyper_state.shape[1:]
    group, _, slots, head = key_cache.shape
    blk_count = lax.axis_size("blk")
    ring = lax.axis_size("y")
    plane = ("zlo", "blk")
    plane_count = lax.axis_size(plane)
    tiles = (width // LANES, LANES)
    f32, bf16 = jnp.float32, jnp.bfloat16

    half = w_gate.shape[1] // 2
    piece = jax.ShapeDtypeStruct((3, half, half), bf16)
    send, mixed, own, sent = pl.pallas_call(
        enter_kernel,
        out_shape=[
            jax.ShapeDtypeStruct((blk_count,) + tiles, f32),
            jax.ShapeDtypeStruct((streams,) + tiles, f32),
            piece,
            piece,
        ],
        in_specs=[VMEM] + [HBM] * 3 + [SMEM] * 2,
        out_specs=[VMEM] * 4,
        scratch_shapes=[pltpu.VMEM((streams,) + tiles, f32), pltpu.SemaphoreType.DMA((6,))],
        cost_estimate=pl.CostEstimate(flops=30 * 10**9, transcendentals=0, bytes_accessed=2**20),
        name="enter",
    )(hyper_state, w_gate, w_up, w_down, width_in, stream_mix)

    def gathered(array):
        return [array] + [
            lax.ppermute(array, "y", [((place + distance) % ring, place) for place in range(ring)])
            for distance in range(1, ring)
        ]

    near = gathered(own)
    far = gathered(lax.ppermute(sent, "zlo", [(0, 1), (1, 0)]))
    group_rows = exchange(send, "blk")

    in_cache_order = lambda cache: jnp.transpose(cache[:, 0], (1, 0, 2)).reshape(slots * group, head)
    pieces = cut(slots * group, 4096)
    steps = cut(slots * group, 8192)
    send = pl.pallas_call(
        functools.partial(attend_kernel, pieces=pieces, steps=steps),
        out_shape=jax.ShapeDtypeStruct((group,) + tiles, f32),
        in_specs=[VMEM, SMEM] + [HBM] * 4,
        out_specs=VMEM,
        scratch_shapes=[
            pltpu.VMEM(attn_in_weight.shape, bf16),
            pltpu.VMEM(attn_out_weight.shape, bf16),
            pltpu.VMEM((slots * group, head), bf16),
            pltpu.VMEM((slots * group, head), bf16),
            pltpu.VMEM((group, slots * group), f32),
            pltpu.SemaphoreType.DMA((2 + 2 * len(pieces),)),
        ],
        compiler_params=pltpu.CompilerParams(vmem_limit_bytes=50 * 2**20),
        cost_estimate=pl.CostEstimate(flops=3 * 10**12, transcendentals=0, bytes_accessed=20 * 2**20),
        name="attend",
    )(
        group_rows,
        lengths,
        attn_in_weight,
        in_cache_order(key_cache),
        in_cache_order(value_cache),
        attn_out_weight,
    )
    received = exchange(send, "blk")
    received, near = lax.optimization_barrier((received, near))

    send, base = pl.pallas_call(
        middle_kernel,
        out_shape=[
            jax.ShapeDtypeStruct((plane_count,) + tiles, bf16),
            jax.ShapeDtypeStruct((streams,) + tiles, f32),
        ],
        in_specs=[VMEM] * 2 + [SMEM] * 3,
        out_specs=[VMEM] * 2,
        cost_estimate=pl.CostEstimate(flops=2 * 10**9, transcendentals=0, bytes_accessed=2**20),
        compiler_params=pltpu.CompilerParams(vmem_limit_bytes=16 * 2**20),
        name="middle",
    )(received, mixed, width_in, stream_mix, depth_out)
    received = exchange(send, plane)

    send = pl.pallas_call(
        feed_kernel,
        out_shape=jax.ShapeDtypeStruct((plane_count,) + tiles, bf16),
        in_specs=[VMEM] + [HBM] * (2 * ring),
        out_specs=VMEM,
        scratch_shapes=[
            pltpu.VMEM((2 * ring,) + own.shape, bf16),
            pltpu.VMEM((plane_count,) + tiles, f32),
            pltpu.SemaphoreType.DMA((2 * ring,)),
        ],
        compiler_params=pltpu.CompilerParams(vmem_limit_bytes=16 * 2**20),
        name="feed",
    )(received, *near, *far)
    received = exchange(send, plane)

    return pl.pallas_call(
        leave_kernel,
        out_shape=jax.ShapeDtypeStruct(hyper_state.shape, f32),
        in_specs=[VMEM] * 2 + [SMEM],
        out_specs=VMEM,
        scratch_shapes=[pltpu.VMEM((streams,) + tiles, f32)],
        name="leave",
    )(received, base, depth_out)


def solution(mesh):
    req_count = mesh.shape["req"]
    blk_count = mesh.shape["blk"]
    fine = Mesh(mesh.devices.reshape(2, req_count // 2, blk_count), ("zlo", "y", "blk"))
    req = ("zlo", "y")
    everyone = P(("zlo", "y", "blk"), None, None)
    placed = (
        everyone,
        P(req),
        P(req, "blk", None, None),
        P(req, "blk", None, None),
        P(None, None, "blk"),
        P("blk", None),
        P(req, "blk"),
        P(req, "blk"),
        P("blk", req),
        P(),
        P(),
        P(),
    )
    return jax.shard_map(
        on_device, mesh=fine, in_specs=placed, out_specs=everyone, check_vma=False
    )
```

```python
import functools
import math

import jax
import jax.numpy as jnp
from jax import lax
from jax.experimental import pallas as pl
from jax.experimental.pallas import tpu as pltpu
from jax.sharding import Mesh, PartitionSpec as P

LANES = 128
FAR_BELOW = -1e30
DEPTH = 12
VMEM = pl.BlockSpec(memory_space=pltpu.VMEM)
SMEM = pl.BlockSpec(memory_space=pltpu.SMEM)
HBM = pl.BlockSpec(memory_space=pltpu.HBM)


def normalize(values):
    count = values.shape[0] * values.shape[1]
    center = values - jnp.sum(values, keepdims=True) / count
    spread = jnp.sum(center * center, keepdims=True) / count
    return center * lax.rsqrt(spread + 1e-05)


def enter_kernel(
    state_ref,
    gate_hbm,
    up_hbm,
    down_hbm,
    width_ref,
    mix_ref,
    send_ref,
    mixed_ref,
    own_ref,
    sent_ref,
    tiles,
    sems,
):
    half = own_ref.shape[1]
    side = lax.axis_index("zlo")
    copies = []
    for index, (target, which) in enumerate(((sent_ref, 1 - side), (own_ref, side))):
        begin = pl.multiple_of(which * half, half)
        copies += [
            pltpu.make_async_copy(gate_hbm.at[:, pl.ds(begin, half)], target.at[0], sems.at[3 * index]),
            pltpu.make_async_copy(up_hbm.at[:, pl.ds(begin, half)], target.at[1], sems.at[3 * index + 1]),
            pltpu.make_async_copy(down_hbm.at[pl.ds(begin, half), :], target.at[2], sems.at[3 * index + 2]),
        ]
    for copy in copies:
        copy.start()
    streams, rows = tiles.shape[0], tiles.shape[1]
    for row in range(rows):
        tiles[:, row, :] = state_ref[0, :, row * LANES : (row + 1) * LANES]
    state = [tiles[stream] for stream in range(streams)]
    combined = sum(width_ref[0, stream] * state[stream] for stream in range(streams))
    normed = normalize(combined).astype(send_ref.dtype)
    send_ref[...] = jnp.broadcast_to(normed[None], send_ref.shape)
    for target in range(streams):
        mixed_ref[target] = sum(mix_ref[0, stream, target] * state[stream] for stream in range(streams))
    for copy in copies:
        copy.wait()


def turn_tables(lengths):
    head = lengths.shape[1]
    place = lax.broadcasted_iota(jnp.int32, lengths.shape, 1)
    index = (place % (head // 2)).astype(jnp.float32)
    freqs = jnp.exp(index * (-2.0 * math.log(10000.0) / head))
    angles = lengths.astype(jnp.float32) * freqs
    sine = jnp.sin(angles)
    return jnp.cos(angles), jnp.where(place < head // 2, -sine, sine)


def attend_kernel(
    rows_ref,
    length_ref,
    weight_hbm,
    keys_hbm,
    values_hbm,
    out_weight_hbm,
    send_ref,
    weight_ref,
    out_weight_ref,
    keys,
    values,
    scores,
    tiles,
    sems,
    *,
    pieces,
    steps,
):
    queue = [pltpu.make_async_copy(weight_hbm, weight_ref, sems.at[0])]
    for source, target in ((keys_hbm, keys), (values_hbm, values)):
        for begin, size in pieces:
            queue.append(
                pltpu.make_async_copy(
                    source.at[pl.ds(begin, size)],
                    target.at[pl.ds(begin, size)],
                    sems.at[len(queue)],
                )
            )
    queue.append(pltpu.make_async_copy(out_weight_hbm, out_weight_ref, sems.at[len(queue)]))
    waited = iter(range(len(queue)))

    def arrive():
        index = next(waited)
        queue[index].wait()
        if index + DEPTH < len(queue):
            queue[index + DEPTH].start()

    for copy in queue[:DEPTH]:
        copy.start()

    group = rows_ref.shape[0]
    head = keys.shape[1]
    request = lax.broadcasted_iota(jnp.int32, (group, head), 0)
    lengths = jnp.zeros((group, head), jnp.int32)
    for row in range(group):
        lengths = jnp.where(request == row, length_ref[row], lengths)
    cosine, sine = turn_tables(lengths)
    tiles[...] = rows_ref[...].astype(jnp.float32)
    rows = jnp.concatenate([tiles[:, row, :] for row in range(tiles.shape[1])], axis=1)
    rows = rows.astype(jnp.bfloat16)
    arrive()
    projected = [
        jnp.dot(rows, weight_ref[index], preferred_element_type=jnp.float32) for index in range(3)
    ]

    def rotate(part):
        turned = pltpu.roll(part, head // 2, 1)
        return (part * cosine + turned * sine).astype(jnp.bfloat16)

    query = rotate(projected[0])
    key_new = rotate(projected[1])
    value_new = projected[2].astype(jnp.bfloat16)
    scale = head ** (-0.5)
    own = jnp.sum(
        query.astype(jnp.float32) * key_new.astype(jnp.float32), axis=1, keepdims=True
    )
    length = lengths[:, :1]
    peak = own

    def within(begin, size):
        return [piece for piece in pieces if begin <= piece[0] < begin + size]

    for begin, size in steps:
        for _ in within(begin, size):
            arrive()
        part = lax.dot_general(
            query,
            keys[begin : begin + size, :],
            (((1,), (1,)), ((), ())),
            preferred_element_type=jnp.float32,
        )
        place = lax.broadcasted_iota(jnp.int32, part.shape, 1)
        mine = place % group == lax.broadcasted_iota(jnp.int32, part.shape, 0)
        inside = place < (length * group - begin)
        part = jnp.where(mine & inside, part, FAR_BELOW)
        scores[:, begin : begin + size] = part
        peak = jnp.maximum(peak, jnp.max(part, axis=1, keepdims=True))

    own_share = jnp.exp((own - peak) * scale)
    denom = own_share
    mixed = own_share * value_new.astype(jnp.float32)
    for begin, size in steps:
        share = jnp.exp((scores[:, begin : begin + size] - peak) * scale)
        denom = denom + jnp.sum(share, axis=1, keepdims=True)
        for _ in within(begin, size):
            arrive()
        mixed = mixed + jnp.dot(
            share.astype(jnp.bfloat16),
            values[begin : begin + size, :],
            preferred_element_type=jnp.float32,
        )
    attended = (mixed / denom).astype(jnp.bfloat16)
    arrive()
    part = jnp.dot(attended, out_weight_ref[...], preferred_element_type=jnp.float32)
    for row in range(tiles.shape[1]):
        tiles[:, row, :] = part[:, row * LANES : (row + 1) * LANES]
    send_ref[...] = tiles[...].astype(send_ref.dtype)


def middle_kernel(received_ref, mixed_ref, width_ref, mix_ref, depth_ref, send_ref, base_ref):
    streams = mixed_ref.shape[0]
    attn_out = jnp.sum(received_ref[...].astype(jnp.float32), axis=0)
    state = [mixed_ref[stream] + depth_ref[0, stream] * attn_out for stream in range(streams)]
    combined = sum(width_ref[1, stream] * state[stream] for stream in range(streams))
    normed = normalize(combined)
    half = normed.shape[0] // 2
    ring = lax.axis_size("y")
    shift = lax.rem((ring - lax.axis_index("y")) * (half // ring), half)
    first = pltpu.roll(normed[:half], shift, 0)
    second = pltpu.roll(normed[half:], shift, 0)
    count = send_ref.shape[0] // 2
    straight = jnp.concatenate([first, second], axis=0).astype(send_ref.dtype)
    crossed = jnp.concatenate([second, first], axis=0).astype(send_ref.dtype)
    shape = (count,) + straight.shape
    send_ref[:count] = jnp.broadcast_to(straight[None], shape)
    send_ref[count:] = jnp.broadcast_to(crossed[None], shape)
    for target in range(streams):
        base_ref[target] = sum(mix_ref[1, stream, target] * state[stream] for stream in range(streams))


def feed_kernel(received_ref, *refs):
    weight_hbms, (send_ref, weights, tiles, sems) = refs[:-4], refs[-4:]
    copies = [
        pltpu.make_async_copy(source, weights.at[index], sems.at[index])
        for index, source in enumerate(weight_hbms)
    ]
    for copy in copies:
        copy.start()
    tiles[...] = received_ref[...].astype(jnp.float32)
    step = weights.shape[2] // LANES
    gate = 0.0
    upward = 0.0
    for index, copy in enumerate(copies):
        piece = jnp.concatenate(
            [tiles[:, index * step + row, :] for row in range(step)], axis=1
        ).astype(jnp.bfloat16)
        copy.wait()
        gate = gate + jnp.dot(piece, weights[index, 0], preferred_element_type=jnp.float32)
        upward = upward + jnp.dot(piece, weights[index, 1], preferred_element_type=jnp.float32)
    hidden = (gate / (1.0 + jnp.exp(-gate)) * upward).astype(jnp.bfloat16)
    for index in range(len(copies)):
        down = jnp.dot(hidden, weights[index, 2], preferred_element_type=jnp.float32)
        for row in range(step):
            tiles[:, index * step + row, :] = down[:, row * LANES : (row + 1) * LANES]
    send_ref[...] = tiles[...].astype(send_ref.dtype)


def leave_kernel(received_ref, base_ref, depth_ref, out_ref, tiles):
    count = received_ref.shape[0] // 2
    straight = jnp.sum(received_ref[:count].astype(jnp.float32), axis=0)
    crossed = jnp.sum(received_ref[count:].astype(jnp.float32), axis=0)
    half = straight.shape[0] // 2
    step = half // lax.axis_size("y")
    shift = lax.axis_index("y") * step
    first = pltpu.roll(straight[:half] + crossed[half:], shift, 0)
    second = pltpu.roll(straight[half:] + crossed[:half], shift, 0)
    mlp_out = jnp.concatenate([first, second], axis=0)
    for stream in range(tiles.shape[0]):
        tiles[stream] = base_ref[stream] + depth_ref[1, stream] * mlp_out
    for row in range(tiles.shape[1]):
        out_ref[0, :, row * LANES : (row + 1) * LANES] = tiles[:, row, :]


def cut(total, size):
    return [(begin, min(size, total - begin)) for begin in range(0, total, size)]


def exchange(rows, axes):
    return lax.all_to_all(rows, axes, split_axis=0, concat_axis=0, tiled=True)


def on_device(
    hyper_state,
    lengths,
    key_cache,
    value_cache,
    attn_in_weight,
    attn_out_weight,
    w_gate,
    w_up,
    w_down,
    width_in,
    stream_mix,
    depth_out,
):
    streams, width = hyper_state.shape[1:]
    group, _, slots, head = key_cache.shape
    blk_count = lax.axis_size("blk")
    ring = lax.axis_size("y")
    plane = ("zlo", "blk")
    plane_count = lax.axis_size(plane)
    tiles = (width // LANES, LANES)
    f32, bf16 = jnp.float32, jnp.bfloat16

    half = w_gate.shape[1] // 2
    piece = jax.ShapeDtypeStruct((3, half, half), bf16)
    send, mixed, own, sent = pl.pallas_call(
        enter_kernel,
        out_shape=[
            jax.ShapeDtypeStruct((blk_count,) + tiles, bf16),
            jax.ShapeDtypeStruct((streams,) + tiles, f32),
            piece,
            piece,
        ],
        in_specs=[VMEM] + [HBM] * 3 + [SMEM] * 2,
        out_specs=[VMEM] * 4,
        scratch_shapes=[pltpu.VMEM((streams,) + tiles, f32), pltpu.SemaphoreType.DMA((6,))],
        cost_estimate=pl.CostEstimate(flops=30 * 10**9, transcendentals=0, bytes_accessed=2**20),
        name="enter",
    )(hyper_state, w_gate, w_up, w_down, width_in, stream_mix)

    def gathered(array):
        return [array] + [
            lax.ppermute(array, "y", [((place + distance) % ring, place) for place in range(ring)])
            for distance in range(1, ring)
        ]

    near = gathered(own)
    far = gathered(lax.ppermute(sent, "zlo", [(0, 1), (1, 0)]))
    group_rows = exchange(send, "blk")

    in_cache_order = lambda cache: jnp.transpose(cache[:, 0], (1, 0, 2)).reshape(slots * group, head)
    pieces = cut(slots * group, 4096)
    steps = cut(slots * group, 8192)
    send = pl.pallas_call(
        functools.partial(attend_kernel, pieces=pieces, steps=steps),
        out_shape=jax.ShapeDtypeStruct((group,) + tiles, bf16),
        in_specs=[VMEM, SMEM] + [HBM] * 4,
        out_specs=VMEM,
        scratch_shapes=[
            pltpu.VMEM(attn_in_weight.shape, bf16),
            pltpu.VMEM(attn_out_weight.shape, bf16),
            pltpu.VMEM((slots * group, head), bf16),
            pltpu.VMEM((slots * group, head), bf16),
            pltpu.VMEM((group, slots * group), f32),
            pltpu.VMEM((group,) + tiles, f32),
            pltpu.SemaphoreType.DMA((2 + 2 * len(pieces),)),
        ],
        compiler_params=pltpu.CompilerParams(vmem_limit_bytes=50 * 2**20),
        cost_estimate=pl.CostEstimate(flops=3 * 10**12, transcendentals=0, bytes_accessed=20 * 2**20),
        name="attend",
    )(
        group_rows,
        lengths,
        attn_in_weight,
        in_cache_order(key_cache),
        in_cache_order(value_cache),
        attn_out_weight,
    )
    received = exchange(send, "blk")
    received, near = lax.optimization_barrier((received, near))

    send, base = pl.pallas_call(
        middle_kernel,
        out_shape=[
            jax.ShapeDtypeStruct((plane_count,) + tiles, bf16),
            jax.ShapeDtypeStruct((streams,) + tiles, f32),
        ],
        in_specs=[VMEM] * 2 + [SMEM] * 3,
        out_specs=[VMEM] * 2,
        cost_estimate=pl.CostEstimate(flops=2 * 10**9, transcendentals=0, bytes_accessed=2**20),
        compiler_params=pltpu.CompilerParams(vmem_limit_bytes=16 * 2**20),
        name="middle",
    )(received, mixed, width_in, stream_mix, depth_out)
    received = exchange(send, plane)

    send = pl.pallas_call(
        feed_kernel,
        out_shape=jax.ShapeDtypeStruct((plane_count,) + tiles, bf16),
        in_specs=[VMEM] + [HBM] * (2 * ring),
        out_specs=VMEM,
        scratch_shapes=[
            pltpu.VMEM((2 * ring,) + own.shape, bf16),
            pltpu.VMEM((plane_count,) + tiles, f32),
            pltpu.SemaphoreType.DMA((2 * ring,)),
        ],
        compiler_params=pltpu.CompilerParams(vmem_limit_bytes=16 * 2**20),
        name="feed",
    )(received, *near, *far)
    received = exchange(send, plane)

    return pl.pallas_call(
        leave_kernel,
        out_shape=jax.ShapeDtypeStruct(hyper_state.shape, f32),
        in_specs=[VMEM] * 2 + [SMEM],
        out_specs=VMEM,
        scratch_shapes=[pltpu.VMEM((streams,) + tiles, f32)],
        name="leave",
    )(received, base, depth_out)


def solution(mesh):
    req_count = mesh.shape["req"]
    blk_count = mesh.shape["blk"]
    fine = Mesh(mesh.devices.reshape(2, req_count // 2, blk_count), ("zlo", "y", "blk"))
    req = ("zlo", "y")
    everyone = P(("zlo", "y", "blk"), None, None)
    placed = (
        everyone,
        P(req),
        P(req, "blk", None, None),
        P(req, "blk", None, None),
        P(None, None, "blk"),
        P("blk", None),
        P(req, "blk"),
        P(req, "blk"),
        P("blk", req),
        P(),
        P(),
        P(),
    )
    return jax.shard_map(
        on_device, mesh=fine, in_specs=placed, out_specs=everyone, check_vma=False
    )
```

```python
import functools
import math

import jax
import jax.numpy as jnp
from jax import lax
from jax.experimental import pallas as pl
from jax.experimental.pallas import tpu as pltpu
from jax.sharding import Mesh, PartitionSpec as P

LANES = 128
FAR_BELOW = -1e30
DEPTH = 12
VMEM = pl.BlockSpec(memory_space=pltpu.VMEM)
SMEM = pl.BlockSpec(memory_space=pltpu.SMEM)
HBM = pl.BlockSpec(memory_space=pltpu.HBM)


def normalize(values):
    count = values.shape[0] * values.shape[1]
    center = values - jnp.sum(values, keepdims=True) / count
    spread = jnp.sum(center * center, keepdims=True) / count
    return center * lax.rsqrt(spread + 1e-05)


def enter_kernel(
    state_ref,
    gate_hbm,
    up_hbm,
    down_hbm,
    width_ref,
    mix_ref,
    send_ref,
    mixed_ref,
    own_ref,
    sent_ref,
    tiles,
    sems,
):
    half = own_ref.shape[1]
    side = lax.axis_index("zlo")
    copies = []
    for index, (target, which) in enumerate(((sent_ref, 1 - side), (own_ref, side))):
        begin = pl.multiple_of(which * half, half)
        copies += [
            pltpu.make_async_copy(gate_hbm.at[:, pl.ds(begin, half)], target.at[0], sems.at[3 * index]),
            pltpu.make_async_copy(up_hbm.at[:, pl.ds(begin, half)], target.at[1], sems.at[3 * index + 1]),
            pltpu.make_async_copy(down_hbm.at[pl.ds(begin, half), :], target.at[2], sems.at[3 * index + 2]),
        ]
    for copy in copies:
        copy.start()
    streams, rows = mixed_ref.shape[0], tiles.shape[1]
    for row in range(rows):
        tiles[:streams, row, :] = state_ref[0, :, row * LANES : (row + 1) * LANES]
    state = [tiles[stream] for stream in range(streams)]
    combined = sum(width_ref[0, stream] * state[stream] for stream in range(streams))
    normed = normalize(combined).astype(send_ref.dtype)
    send_ref[...] = jnp.broadcast_to(normed[None], send_ref.shape)
    for target in range(streams):
        mixed_ref[target] = sum(mix_ref[0, stream, target] * state[stream] for stream in range(streams))
    for copy in copies:
        copy.wait()


def turn_tables(lengths):
    head = lengths.shape[1]
    place = lax.broadcasted_iota(jnp.int32, lengths.shape, 1)
    index = (place % (head // 2)).astype(jnp.float32)
    freqs = jnp.exp(index * (-2.0 * math.log(10000.0) / head))
    angles = lengths.astype(jnp.float32) * freqs
    sine = jnp.sin(angles)
    return jnp.cos(angles), jnp.where(place < head // 2, -sine, sine)


def attend_kernel(
    rows_ref,
    length_ref,
    weight_hbm,
    keys_hbm,
    values_hbm,
    out_weight_hbm,
    send_ref,
    weight_ref,
    out_weight_ref,
    keys,
    values,
    scores,
    tiles,
    sems,
    *,
    pieces,
    steps,
):
    queue = [pltpu.make_async_copy(weight_hbm, weight_ref, sems.at[0])]
    for source, target in ((keys_hbm, keys), (values_hbm, values)):
        for begin, size in pieces:
            queue.append(
                pltpu.make_async_copy(
                    source.at[pl.ds(begin, size)],
                    target.at[pl.ds(begin, size)],
                    sems.at[len(queue)],
                )
            )
    queue.append(pltpu.make_async_copy(out_weight_hbm, out_weight_ref, sems.at[len(queue)]))
    waited = iter(range(len(queue)))

    def arrive():
        index = next(waited)
        queue[index].wait()
        if index + DEPTH < len(queue):
            queue[index + DEPTH].start()

    for copy in queue[:DEPTH]:
        copy.start()

    group = rows_ref.shape[0]
    head = keys.shape[1]
    request = lax.broadcasted_iota(jnp.int32, (group, head), 0)
    lengths = jnp.zeros((group, head), jnp.int32)
    for row in range(group):
        lengths = jnp.where(request == row, length_ref[row], lengths)
    cosine, sine = turn_tables(lengths)
    tiles[...] = rows_ref[...].astype(jnp.float32)
    rows = jnp.concatenate([tiles[:, row, :] for row in range(tiles.shape[1])], axis=1)
    rows = rows.astype(jnp.bfloat16)
    arrive()
    projected = [
        jnp.dot(rows, weight_ref[index], preferred_element_type=jnp.float32) for index in range(3)
    ]

    def rotate(part):
        turned = pltpu.roll(part, head // 2, 1)
        return (part * cosine + turned * sine).astype(jnp.bfloat16)

    query = rotate(projected[0])
    key_new = rotate(projected[1])
    value_new = projected[2].astype(jnp.bfloat16)
    scale = head ** (-0.5)
    own = jnp.sum(
        query.astype(jnp.float32) * key_new.astype(jnp.float32), axis=1, keepdims=True
    )
    length = lengths[:, :1]
    peak = own

    def within(begin, size):
        return [piece for piece in pieces if begin <= piece[0] < begin + size]

    for begin, size in steps:
        for _ in within(begin, size):
            arrive()
        part = lax.dot_general(
            query,
            keys[begin : begin + size, :],
            (((1,), (1,)), ((), ())),
            preferred_element_type=jnp.float32,
        )
        place = lax.broadcasted_iota(jnp.int32, part.shape, 1)
        mine = place % group == lax.broadcasted_iota(jnp.int32, part.shape, 0)
        inside = place < (length * group - begin)
        part = jnp.where(mine & inside, part, FAR_BELOW)
        scores[:, begin : begin + size] = part
        peak = jnp.maximum(peak, jnp.max(part, axis=1, keepdims=True))

    own_share = jnp.exp((own - peak) * scale)
    denom = own_share
    mixed = own_share * value_new.astype(jnp.float32)
    for begin, size in steps:
        share = jnp.exp((scores[:, begin : begin + size] - peak) * scale)
        denom = denom + jnp.sum(share, axis=1, keepdims=True)
        for _ in within(begin, size):
            arrive()
        mixed = mixed + jnp.dot(
            share.astype(jnp.bfloat16),
            values[begin : begin + size, :],
            preferred_element_type=jnp.float32,
        )
    attended = (mixed / denom).astype(jnp.bfloat16)
    arrive()
    part = jnp.dot(attended, out_weight_ref[...], preferred_element_type=jnp.float32)
    for row in range(tiles.shape[1]):
        tiles[:, row, :] = part[:, row * LANES : (row + 1) * LANES]
    send_ref[...] = tiles[...].astype(send_ref.dtype)


def middle_kernel(received_ref, mixed_ref, width_ref, mix_ref, depth_ref, send_ref, base_ref):
    streams = mixed_ref.shape[0]
    attn_out = jnp.sum(received_ref[...].astype(jnp.float32), axis=0)
    state = [mixed_ref[stream] + depth_ref[0, stream] * attn_out for stream in range(streams)]
    combined = sum(width_ref[1, stream] * state[stream] for stream in range(streams))
    normed = normalize(combined)
    half = normed.shape[0] // 2
    ring = lax.axis_size("y")
    shift = lax.rem((ring - lax.axis_index("y")) * (half // ring), half)
    first = pltpu.roll(normed[:half], shift, 0)
    second = pltpu.roll(normed[half:], shift, 0)
    count = send_ref.shape[0] // 2
    straight = jnp.concatenate([first, second], axis=0).astype(send_ref.dtype)
    crossed = jnp.concatenate([second, first], axis=0).astype(send_ref.dtype)
    shape = (count,) + straight.shape
    send_ref[:count] = jnp.broadcast_to(straight[None], shape)
    send_ref[count:] = jnp.broadcast_to(crossed[None], shape)
    for target in range(streams):
        base_ref[target] = sum(mix_ref[1, stream, target] * state[stream] for stream in range(streams))


def feed_kernel(received_ref, *refs):
    weight_hbms, (send_ref, weights, tiles, sems) = refs[:-4], refs[-4:]
    copies = [
        pltpu.make_async_copy(source, weights.at[index], sems.at[index])
        for index, source in enumerate(weight_hbms)
    ]
    for copy in copies:
        copy.start()
    tiles[...] = received_ref[...].astype(jnp.float32)
    step = weights.shape[2] // LANES
    gate = 0.0
    upward = 0.0
    for index, copy in enumerate(copies):
        piece = jnp.concatenate(
            [tiles[:, index * step + row, :] for row in range(step)], axis=1
        ).astype(jnp.bfloat16)
        copy.wait()
        gate = gate + jnp.dot(piece, weights[index, 0], preferred_element_type=jnp.float32)
        upward = upward + jnp.dot(piece, weights[index, 1], preferred_element_type=jnp.float32)
    hidden = (gate / (1.0 + jnp.exp(-gate)) * upward).astype(jnp.bfloat16)
    for index in range(len(copies)):
        down = jnp.dot(hidden, weights[index, 2], preferred_element_type=jnp.float32)
        for row in range(step):
            tiles[:, index * step + row, :] = down[:, row * LANES : (row + 1) * LANES]
    send_ref[...] = tiles[...].astype(send_ref.dtype)


def leave_kernel(received_ref, base_ref, depth_ref, out_ref, tiles):
    count = received_ref.shape[0] // 2
    straight = jnp.sum(received_ref[:count].astype(jnp.float32), axis=0)
    crossed = jnp.sum(received_ref[count:].astype(jnp.float32), axis=0)
    half = straight.shape[0] // 2
    step = half // lax.axis_size("y")
    shift = lax.axis_index("y") * step
    first = pltpu.roll(straight[:half] + crossed[half:], shift, 0)
    second = pltpu.roll(straight[half:] + crossed[:half], shift, 0)
    mlp_out = jnp.concatenate([first, second], axis=0)
    streams = base_ref.shape[0]
    for stream in range(streams):
        tiles[stream] = base_ref[stream] + depth_ref[1, stream] * mlp_out
    for row in range(tiles.shape[1]):
        out_ref[0, :, row * LANES : (row + 1) * LANES] = tiles[:streams, row, :]


def cut(total, size):
    return [(begin, min(size, total - begin)) for begin in range(0, total, size)]


def exchange(rows, axes):
    return lax.all_to_all(rows, axes, split_axis=0, concat_axis=0, tiled=True)


def on_device(
    hyper_state,
    lengths,
    key_cache,
    value_cache,
    attn_in_weight,
    attn_out_weight,
    w_gate,
    w_up,
    w_down,
    width_in,
    stream_mix,
    depth_out,
):
    streams, width = hyper_state.shape[1:]
    group, _, slots, head = key_cache.shape
    blk_count = lax.axis_size("blk")
    ring = lax.axis_size("y")
    plane = ("zlo", "blk")
    plane_count = lax.axis_size(plane)
    tiles = (width // LANES, LANES)
    f32, bf16 = jnp.float32, jnp.bfloat16

    half = w_gate.shape[1] // 2
    piece = jax.ShapeDtypeStruct((3, half, half), bf16)
    send, mixed, own, sent = pl.pallas_call(
        enter_kernel,
        out_shape=[
            jax.ShapeDtypeStruct((blk_count,) + tiles, bf16),
            jax.ShapeDtypeStruct((streams,) + tiles, f32),
            piece,
            piece,
        ],
        in_specs=[VMEM] + [HBM] * 3 + [SMEM] * 2,
        out_specs=[VMEM] * 4,
        scratch_shapes=[pltpu.VMEM((8 * pl.cdiv(streams, 8),) + tiles, f32), pltpu.SemaphoreType.DMA((6,))],
        cost_estimate=pl.CostEstimate(flops=30 * 10**9, transcendentals=0, bytes_accessed=2**20),
        name="enter",
    )(hyper_state, w_gate, w_up, w_down, width_in, stream_mix)

    def gathered(array):
        return [array] + [
            lax.ppermute(array, "y", [((place + distance) % ring, place) for place in range(ring)])
            for distance in range(1, ring)
        ]

    near = gathered(own)
    far = gathered(lax.ppermute(sent, "zlo", [(0, 1), (1, 0)]))
    group_rows = exchange(send, "blk")

    in_cache_order = lambda cache: jnp.transpose(cache[:, 0], (1, 0, 2)).reshape(slots * group, head)
    pieces = cut(slots * group, 4096)
    steps = cut(slots * group, 8192)
    send = pl.pallas_call(
        functools.partial(attend_kernel, pieces=pieces, steps=steps),
        out_shape=jax.ShapeDtypeStruct((group,) + tiles, bf16),
        in_specs=[VMEM, SMEM] + [HBM] * 4,
        out_specs=VMEM,
        scratch_shapes=[
            pltpu.VMEM(attn_in_weight.shape, bf16),
            pltpu.VMEM(attn_out_weight.shape, bf16),
            pltpu.VMEM((slots * group, head), bf16),
            pltpu.VMEM((slots * group, head), bf16),
            pltpu.VMEM((group, LANES * pl.cdiv(slots * group, LANES)), f32),
            pltpu.VMEM((group,) + tiles, f32),
            pltpu.SemaphoreType.DMA((2 + 2 * len(pieces),)),
        ],
        compiler_params=pltpu.CompilerParams(vmem_limit_bytes=50 * 2**20),
        cost_estimate=pl.CostEstimate(flops=3 * 10**12, transcendentals=0, bytes_accessed=20 * 2**20),
        name="attend",
    )(
        group_rows,
        lengths,
        attn_in_weight,
        in_cache_order(key_cache),
        in_cache_order(value_cache),
        attn_out_weight,
    )
    received = exchange(send, "blk")
    received, near = lax.optimization_barrier((received, near))

    send, base = pl.pallas_call(
        middle_kernel,
        out_shape=[
            jax.ShapeDtypeStruct((plane_count,) + tiles, bf16),
            jax.ShapeDtypeStruct((streams,) + tiles, f32),
        ],
        in_specs=[VMEM] * 2 + [SMEM] * 3,
        out_specs=[VMEM] * 2,
        cost_estimate=pl.CostEstimate(flops=2 * 10**9, transcendentals=0, bytes_accessed=2**20),
        compiler_params=pltpu.CompilerParams(vmem_limit_bytes=16 * 2**20),
        name="middle",
    )(received, mixed, width_in, stream_mix, depth_out)
    received = exchange(send, plane)

    send = pl.pallas_call(
        feed_kernel,
        out_shape=jax.ShapeDtypeStruct((plane_count,) + tiles, bf16),
        in_specs=[VMEM] + [HBM] * (2 * ring),
        out_specs=VMEM,
        scratch_shapes=[
            pltpu.VMEM((2 * ring,) + own.shape, bf16),
            pltpu.VMEM((plane_count,) + tiles, f32),
            pltpu.SemaphoreType.DMA((2 * ring,)),
        ],
        compiler_params=pltpu.CompilerParams(vmem_limit_bytes=16 * 2**20),
        name="feed",
    )(received, *near, *far)
    received = exchange(send, plane)

    return pl.pallas_call(
        leave_kernel,
        out_shape=jax.ShapeDtypeStruct(hyper_state.shape, f32),
        in_specs=[VMEM] * 2 + [SMEM],
        out_specs=VMEM,
        scratch_shapes=[pltpu.VMEM((8 * pl.cdiv(streams, 8),) + tiles, f32)],
        name="leave",
    )(received, base, depth_out)


def solution(mesh):
    req_count = mesh.shape["req"]
    blk_count = mesh.shape["blk"]
    fine = Mesh(mesh.devices.reshape(2, req_count // 2, blk_count), ("zlo", "y", "blk"))
    req = ("zlo", "y")
    everyone = P(("zlo", "y", "blk"), None, None)
    placed = (
        everyone,
        P(req),
        P(req, "blk", None, None),
        P(req, "blk", None, None),
        P(None, None, "blk"),
        P("blk", None),
        P(req, "blk"),
        P(req, "blk"),
        P("blk", req),
        P(),
        P(),
        P(),
    )
    return jax.shard_map(
        on_device, mesh=fine, in_specs=placed, out_specs=everyone, check_vma=False
    )
```
